32 devices in a mesh: dp: 8 (over z, y), expert: 4 (over x, core).
Axes of the slice: x: 2, y: 2, z: 4, core: 2. Of those that a mesh axis runs over, the one named last changes fastest.
Arguments:
- inputs: bfloat16 [64, 256, 1024], P('expert', 'dp'), may hold values from -6 to 6
- cotangent: bfloat16 [64, 256, 1024], P('expert', 'dp'), may hold values from -6 to 6
- seq_lengths: int32 [64], P('expert'), may hold values from 1 to 256, 10240 in all
- deal_perm: int32 [8, 8], P('expert'), may hold values from 0 to 7, each once within a row
- routes: int32 [64, 256, 2], P(('dp', 'expert')), may hold values from 0 to 3, all different within a row
- route_order: int32 [64, 512], P(('dp', 'expert')), may hold values from 0 to 511, each once within a row
- qkv_weight: bfloat16 [1024, 3072], P(('dp', 'expert')), may hold values from -0.1875 to 0.1875
- out_weight: bfloat16 [1024, 1024], P(('dp', 'expert')), may hold values from -0.75 to 0.75
- attention_gain: bfloat16 [1024], P(('dp', 'expert')), may hold values from 0.5 to 1.5
- expert_gain: bfloat16 [1024], P(('dp', 'expert')), may hold values from 0.5 to 1.5
- router_weight: bfloat16 [1024, 4], P(('dp', 'expert')), may hold values from -0.1875 to 0.1875
- position_bias: bfloat16 [512], P(('dp', 'expert')), may hold values from -4 to 4
- expert_in: bfloat16 [4, 1024, 5632], P('expert'), may hold values from -0.1875 to 0.1875
- expert_out: bfloat16 [4, 2816, 1024], P('expert'), may hold values from -1.25 to 1.25
Outputs:
- output: bfloat16 [64, 256, 1024], P('expert', 'dp')
- input_grad: bfloat16 [64, 256, 1024], P('expert', 'dp')
- qkv_weight_grad: float32 [1024, 3072], P(('dp', 'expert'))
- out_weight_grad: float32 [1024, 1024], P(('dp', 'expert'))
- attention_gain_grad: float32 [1024], P(('dp', 'expert'))
- expert_gain_grad: float32 [1024], P(('dp', 'expert'))
- router_weight_grad: float32 [1024, 4], P(('dp', 'expert'))
- position_bias_grad: float32 [512], P(('dp', 'expert'))
- expert_in_grad: float32 [4, 1024, 5632], P('expert', 'dp')
- expert_out_grad: float32 [4, 2816, 1024], P('expert', 'dp')
The draws below stay inside these ranges and needn't reach their ends.
Inputs may be any that keep to these rules, and one draw needn't show every extreme that they name: `seq_lengths`: lengths of the stored sequences; positions at or past a length are padding. `deal_perm`: row b * 2 + m lists every dp index once; entry a names which sequence of that group the dp index a takes. The two experts of a position differ; routes of padding positions are ignored. `route_order`: each row lists every pair index of its slot once.
All inputs are finite; a program needn't handle non-finite values. No bound on the sum of `seq_lengths` on one device may be relied on, other than what follows from the above.
Results may differ from the reference program's by a relative error of at most 0.024.
Values may be sent and summed in bfloat16 or wider, within the bound.
No kernel may reach another device: no remote copies, remote signals or barrier semaphores. Data moves between devices by JAX's collectives and lax.ppermute only.
A program may use at most 256 MiB of HBM per device.

```python
import math
import jax
import jax.numpy as jnp
import numpy as np
from jax import lax

D = 1024
HEADS = 16
HEAD = 64
FF = 2816
NB = 32
MAXDIST = 128
TOPK = 2
MICRO = 2
SEQ = 256
EXPERTS = 4
CAP = 160
SEQS = 64
N_DP = 8
N_EXPERT = 4


def level_of(own_key, dims, shards, low, high):
    def one(dim, blocks):
        heights = jax.random.uniform(jax.random.fold_in(jax.random.fold_in(own_key, 6), dim), (blocks,), jnp.float32, low / len(shards), high / len(shards))
        return jnp.repeat(jnp.exp(heights), dims[dim] // blocks).reshape((-1,) + (1,) * (len(dims) - dim - 1))

    level = one(*shards[0])
    for cut in shards[1:]:
        level = level * one(*cut)
    return level


def distinct(key, rows, count, top, lift):
    order = jax.random.permutation(jax.random.fold_in(key, 1), count)
    boost = order
    for power in range(3):
        boost = boost * boost // count
    boost = boost * lift // count
    chance = jax.random.randint(jax.random.fold_in(key, 2), (rows, count), 0, 4096) + boost
    sure = jax.random.permutation(jax.random.fold_in(key, 3), rows)[jnp.arange(count) % rows]
    chance = jnp.where(jnp.arange(rows)[:, None] == sure[None, :], 1 << 14, chance)
    priority = chance * count + jnp.arange(count)
    return lax.top_k(priority.astype(jnp.int32), top)[1].astype(jnp.int32)


def split_up(amount, total, most, skew):
    portions = [(1 << 20) // math.isqrt(grade ** skew) + 1 for grade in range(2, amount + 1)]
    spare, given = total - most - (amount - 1), [1] * (amount - 1)
    while spare > 0:
        candidates = [i for i in range(amount - 1) if given[i] < most]
        pool, remaining = sum([portions[i] for i in candidates]), spare
        for i in candidates:
            more = min(most - given[i], max(1, remaining * portions[i] // pool), spare)
            given[i] = given[i] + more
            spare = spare - more
    return np.array([most] + given)


def ragged(own_key, amount, total, limit, skew):
    if amount == 2:
        one = jax.random.randint(own_key, (), max(1, total - limit), min(limit, total - 1) + 1)
        return jnp.stack([one, total - one])
    tallies = jnp.asarray(split_up(amount, total, limit, skew), jnp.int32)
    twos = (amount - 1) // 2
    source_of, receiver = tallies[1:1 + 2 * twos:2], tallies[2:2 + 2 * twos:2]
    margin = jnp.minimum(source_of - 1, limit - receiver)
    shifted = jax.random.randint(jax.random.fold_in(own_key, 1), (twos,), 0, 1 << 20) % (margin + 1)
    tallies = tallies.at[1:1 + 2 * twos:2].set(source_of - shifted).at[2:2 + 2 * twos:2].set(receiver + shifted)
    return tallies[jax.random.permutation(jax.random.fold_in(own_key, 2), amount)]


def normal_values(key, extent, scale, bound, split=(), kind=jnp.bfloat16):
    level = level_of(key, extent, split, -0.22, 0.18) if split else 1.0
    drawn = jax.random.normal(key, extent, jnp.float32) * scale * level
    return jnp.minimum(jnp.maximum(drawn, -bound), bound).astype(kind)


def setup_inputs(seed: int = 0) -> dict:
    key_of = jax.random.split(jax.random.key(seed), 15)
    return {
        "inputs": normal_values(key_of[0], (SEQS, SEQ, D), 1.0, 6.0, ((0, 4), (1, 8))),
        "cotangent": normal_values(key_of[1], (SEQS, SEQ, D), 1.0, 6.0, ((0, 4), (1, 8))),
        "seq_lengths": ragged(key_of[2], SEQS, SEQS * SEQ * 5 // 8, SEQ, 1).astype(jnp.int32),
        "deal_perm": jax.vmap(lambda own: jax.random.permutation(own, N_DP))(jax.random.split(key_of[3], (N_EXPERT * MICRO))).reshape((N_EXPERT * MICRO, N_DP)).astype(jnp.int32),
        "routes": distinct(key_of[4], SEQS * SEQ, EXPERTS, TOPK, 4096).reshape((SEQS, SEQ, TOPK)),
        "route_order": jax.vmap(lambda own: jax.random.permutation(own, TOPK * SEQ))(jax.random.split(key_of[5], SEQS)).reshape((SEQS, TOPK * SEQ)).astype(jnp.int32),
        "qkv_weight": normal_values(key_of[6], (D, 3 * D), D ** -0.5, 0.1875, ((0, 32),)),
        "out_weight": normal_values(key_of[7], (D, D), (D // 16) ** -0.5, 0.75, ((0, 32),)),
        "attention_gain": jnp.clip(1.0 + 0.1 * jax.random.normal(key_of[8], (D,), jnp.float32), 0.5, 1.5).astype(jnp.bfloat16),
        "expert_gain": jnp.clip(1.0 + 0.1 * jax.random.normal(key_of[9], (D,), jnp.float32), 0.5, 1.5).astype(jnp.bfloat16),
        "router_weight": normal_values(key_of[10], (D, EXPERTS), D ** -0.5, 0.1875, ((0, 32),)),
        "position_bias": normal_values(key_of[11], (NB * HEADS,), 1.0, 4.0, ((0, 32),)),
        "expert_in": normal_values(key_of[12], (EXPERTS, D, 2 * FF), D ** -0.5, 0.1875, ((0, 4),)),
        "expert_out": normal_values(key_of[13], (EXPERTS, FF, D), (max(FF // 128, 1)) ** -0.5, 1.25, ((0, 4),)),
    }


EPSILON = 1e-06
HIGHEST = lax.Precision.HIGHEST
MASKED = -1000000000.0

@jax.custom_vjp
def low(v):
    return lax.optimization_barrier(v.astype(jnp.bfloat16)).astype(jnp.float32)

@jax.custom_vjp
def low_back(v):
    return v

def low_keep(v):
    return (low(v), None)

def low_pass(kept, grad):
    return (grad,)

def back_keep(v):
    return (v, None)

def back_low(kept, grad):
    return (low(grad),)
low.defvjp(low_keep, low_pass)
low_back.defvjp(back_keep, back_low)

def bucket_table(length, buckets, reach):
    offset = np.arange(length)[None, :] - np.arange(length)[:, None]
    half = buckets // 2
    exact = half // 2
    distance = np.abs(offset)
    spread = exact + (np.log(np.maximum(distance, 1) / exact) / np.log(reach / exact) * (half - exact)).astype(np.int32)
    spread = np.minimum(spread, half - 1)
    table = (offset > 0).astype(np.int32) * half + np.where(distance < exact, distance, spread)
    return table.astype(np.int32)

def position_onehot(length, buckets, reach):
    table = jnp.asarray(bucket_table(length, buckets, reach))
    return (table[:, :, None] == jnp.arange(buckets, dtype=jnp.int32)[None, None, :]).astype(jnp.float32)

def normalized(hidden, gain):
    return hidden * lax.rsqrt(lax.optimization_barrier(jnp.mean(hidden * hidden, axis=-1, keepdims=True)) + EPSILON) * gain

def gated_units(pre):
    half = pre.shape[-1] // 2
    return jax.nn.gelu(pre[..., :half]) * pre[..., half:]

def route_pairs(pair_expert, pair_order, valid_rows, expert_count, capacity, topk):
    pair_valid = jnp.repeat(valid_rows, topk)
    ordered_expert = pair_expert[pair_order]
    ordered_valid = pair_valid[pair_order]
    matches = ordered_expert[:, None] == jnp.arange(expert_count, dtype=jnp.int32)[None, :]
    counted = (matches & ordered_valid[:, None]).astype(jnp.int32)
    earlier = jnp.cumsum(counted, axis=0, dtype=jnp.int32) - counted
    ordered_rank = lax.optimization_barrier(jnp.sum(earlier * matches.astype(jnp.int32), axis=1, dtype=jnp.int32))
    rank = jnp.zeros(ordered_rank.shape, jnp.int32).at[pair_order].set(ordered_rank)
    kept = pair_valid & (rank < capacity)
    slot = jnp.where(kept, pair_expert * capacity + rank, expert_count * capacity).astype(jnp.int32)
    pair_token = (jnp.arange(pair_expert.shape[0], dtype=jnp.int32) // topk).astype(jnp.int32)
    holder = jnp.zeros((expert_count * capacity + 1,), jnp.int32).at[slot].set(pair_token)[:-1]
    filled = jnp.zeros((expert_count * capacity + 1,), jnp.bool_).at[slot].set(True)[:-1]
    return (kept, slot, holder, filled)

def sequence_forward(params, tokens, length, pair_expert, pair_order):
    qkv_weight, out_weight, attention_gain, expert_gain, router_weight, position_bias, expert_in, expert_out = params
    valid = jnp.arange(SEQ, dtype=jnp.int32) < length
    first = low(normalized(tokens, attention_gain))
    projected = low(low_back(jnp.dot(first, qkv_weight, precision=HIGHEST)))
    queries = projected[:, :D].reshape(SEQ, HEADS, HEAD)
    key_rows = projected[:, D:2 * D].reshape(SEQ, HEADS, HEAD)
    value_rows = projected[:, 2 * D:].reshape(SEQ, HEADS, HEAD)
    bias_heads = jnp.einsum('ijb,bh->hij', position_onehot(SEQ, NB, MAXDIST), position_bias.reshape(NB, HEADS), precision=HIGHEST)
    scores = jnp.einsum('ihd,jhd->hij', queries, key_rows, precision=HIGHEST) * (1.0 / math.sqrt(HEAD)) + bias_heads
    scores = low_back(jnp.where(valid[None, None, :], scores, MASKED))
    weights = low(jax.nn.softmax(scores, axis=-1))
    mixed = low(low_back(jnp.einsum('hij,jhd->ihd', weights, value_rows, precision=HIGHEST).reshape(SEQ, D)))
    residual = tokens + low_back(jnp.dot(mixed, out_weight, precision=HIGHEST))
    second = low(normalized(residual, expert_gain))
    gate_probs = jax.nn.softmax(jnp.dot(second, router_weight, precision=HIGHEST), axis=-1)
    kept, slot, holder, filled = route_pairs(pair_expert, pair_order, valid, EXPERTS, CAP, TOPK)
    dispatched = low_back(jnp.where(filled[:, None], second[holder], 0.0)).reshape(EXPERTS, CAP, D)
    pre = low_back(jnp.einsum('ecd,edf->ecf', dispatched, expert_in, precision=HIGHEST))
    hidden = low(gated_units(pre))
    produced = low(low_back(jnp.einsum('ecf,efd->ecd', hidden, expert_out, precision=HIGHEST))).reshape(EXPERTS * CAP, D)
    choice_onehot = (pair_expert.reshape(SEQ, TOPK)[:, :, None] == jnp.arange(EXPERTS, dtype=jnp.int32)[None, None, :]).astype(jnp.float32)
    pair_prob = lax.optimization_barrier(jnp.sum(choice_onehot * gate_probs[:, None, :], axis=-1))
    pair_weight = jnp.where(kept.reshape(SEQ, TOPK), pair_prob, 0.0)
    picked = produced[jnp.minimum(slot, EXPERTS * CAP - 1)].reshape(SEQ, TOPK, D)
    combined = lax.optimization_barrier(jnp.sum(pair_weight[:, :, None] * picked, axis=1))
    return jnp.where(valid[:, None], residual + combined, 0.0)

def reference(inputs, cotangent, seq_lengths, deal_perm, routes, route_order, qkv_weight, out_weight, attention_gain, expert_gain, router_weight, position_bias, expert_in, expert_out):
    slots = jnp.arange(SEQS, dtype=jnp.int32)
    dp_place = slots // (N_EXPERT * MICRO)
    expert_place = slots // MICRO % N_EXPERT
    micro_place = slots % MICRO
    stored = (expert_place * (MICRO * N_DP) + micro_place * N_DP + deal_perm[expert_place * MICRO + micro_place, dp_place]).astype(jnp.int32)
    tokens = inputs[stored].astype(jnp.float32)
    upstream = cotangent[stored].astype(jnp.float32)
    lengths = seq_lengths[stored]
    pair_experts = routes.reshape(SEQS, SEQ * TOPK)
    params = (qkv_weight.astype(jnp.float32), out_weight.astype(jnp.float32), attention_gain.astype(jnp.float32), expert_gain.astype(jnp.float32), router_weight.astype(jnp.float32), position_bias.astype(jnp.float32), expert_in.astype(jnp.float32), expert_out.astype(jnp.float32))

    def forward(weights_all, tokens_all):

        def one_slot(item):
            return jax.checkpoint(sequence_forward)(weights_all, item[0], item[1], item[2], item[3])
        return lax.map(one_slot, (tokens_all, lengths, pair_experts, route_order))
    produced, pullback = jax.vjp(forward, params, tokens)
    grads, token_grads = pullback(upstream)
    output = jnp.zeros(inputs.shape, jnp.bfloat16).at[stored].set(produced.astype(jnp.bfloat16))
    input_grad = jnp.zeros(inputs.shape, jnp.bfloat16).at[stored].set(token_grads.astype(jnp.bfloat16))
    return (output, input_grad, grads[0], grads[1], grads[2], grads[3], grads[4], grads[5], grads[6], grads[7])
```

```python
import functools
import math

import jax
import jax.numpy as jnp
import numpy as np
from jax import lax
from jax.experimental import pallas as pl
from jax.experimental.pallas import tpu as pltpu
from jax.sharding import PartitionSpec as P

HEADS = 16
NB = 32
MAXDIST = 128
TOPK = 2
EPSILON = 1e-06
MASKED = -1000000000.0
VMEM_LIMIT = 60 * 1024 * 1024
BF16 = jnp.bfloat16
F32 = jnp.float32
I32 = jnp.int32


def bucket_of_offsets(length, buckets, reach):
    offset = np.arange(2 * length) - (length - 1)
    half = buckets // 2
    exact = half // 2
    distance = np.abs(offset)
    spread = exact + (
        np.log(np.maximum(distance, 1) / exact) / np.log(reach / exact) * (half - exact)
    ).astype(np.int32)
    spread = np.minimum(spread, half - 1)
    table = (offset > 0).astype(np.int32) * half + np.where(distance < exact, distance, spread)
    onehot = (table[None, :] == np.arange(buckets)[:, None]).astype(np.float32)
    onehot[:, 2 * length - 1] = 0.0
    return onehot


def params(**more):
    return pltpu.CompilerParams(vmem_limit_bytes=VMEM_LIMIT, **more)


def cost(flops, nbytes):
    return pl.CostEstimate(flops=int(flops), bytes_accessed=int(nbytes), transcendentals=0)


VM = pl.BlockSpec(memory_space=pltpu.VMEM)
SM = pl.BlockSpec(memory_space=pltpu.SMEM)
ANY = pl.BlockSpec(memory_space=pl.ANY)


def div2(v, n):
    return lax.shift_right_logical(v, jnp.full_like(v, n.bit_length() - 1))


def mod2(v, n):
    return lax.bitwise_and(v, jnp.full_like(v, n - 1))


def dot(a, b):
    return jnp.dot(a, b, preferred_element_type=F32)


def dot_nt(a, b):
    return lax.dot_general(a, b, (((1,), (1,)), ((), ())), preferred_element_type=F32)


def dot_tn(a, b):
    return lax.dot_general(a, b, (((0,), (0,)), ((), ())), preferred_element_type=F32)


def pick_kernel(idx_ref, src_ref, out_ref, sems):
    count = out_ref.shape[0]
    copies = [
        pltpu.make_async_copy(src_ref.at[idx_ref[n]], out_ref.at[n], sems.at[n])
        for n in range(count)
    ]
    for c in copies:
        c.start()
    for c in copies:
        c.wait()


def pick_blocks(idx, src):
    return pl.pallas_call(
        pick_kernel,
        out_shape=jax.ShapeDtypeStruct(src.shape, src.dtype),
        in_specs=[SM, ANY],
        out_specs=VM,
        scratch_shapes=[pltpu.SemaphoreType.DMA((src.shape[0],))],
        compiler_params=params(),
        cost_estimate=cost(0, 4 * src.size),
    )(idx, src)


def place_kernel(idx_ref, src_ref, out_ref, sems):
    count = src_ref.shape[0]
    copies = [
        pltpu.make_async_copy(src_ref.at[n], out_ref.at[idx_ref[n]], sems.at[n])
        for n in range(count)
    ]
    for c in copies:
        c.start()
    for c in copies:
        c.wait()


def place_blocks(idx, src):
    return pl.pallas_call(
        place_kernel,
        out_shape=jax.ShapeDtypeStruct(src.shape, src.dtype),
        in_specs=[SM, VM],
        out_specs=ANY,
        scratch_shapes=[pltpu.SemaphoreType.DMA((src.shape[0],))],
        compiler_params=params(),
        cost_estimate=cost(0, 4 * src.size),
    )(idx, src)


def route_kernel(len_ref, er_ref, ec_ref, orow_ref, ocol_ref, srow_ref, scol_ref, *, cap):
    length = len_ref[pl.program_id(0)]
    seq = er_ref.shape[2]
    pairs = TOPK * seq
    order_row = orow_ref[0]
    order_col = ocol_ref[0]
    wide = (seq, pairs)
    tall = (pairs, seq)
    pos_col, pos_row = [], []
    for k in range(TOPK):
        pair = lax.broadcasted_iota(I32, wide, 0) * TOPK + k
        when = lax.broadcasted_iota(I32, wide, 1).astype(F32)
        pos_col.append(jnp.sum(jnp.where(order_row == pair, when, 0.0), axis=1, keepdims=True))
        pair = lax.broadcasted_iota(I32, tall, 1) * TOPK + k
        when = lax.broadcasted_iota(I32, tall, 0).astype(F32)
        pos_row.append(jnp.sum(jnp.where(order_col == pair, when, 0.0), axis=0, keepdims=True))
    square = (seq, seq)
    ahead_lane = lax.broadcasted_iota(I32, square, 1) < length
    ahead_sub = lax.broadcasted_iota(I32, square, 0) < length
    for k in range(TOPK):
        e_col = ec_ref[0, :, k : k + 1]
        e_row = er_ref[0, k : k + 1, :]
        rank_col = jnp.zeros((seq, 1), F32)
        rank_row = jnp.zeros((1, seq), F32)
        for other in range(TOPK):
            o_row = er_ref[0, other : other + 1, :]
            o_col = ec_ref[0, :, other : other + 1]
            before = (o_row == e_col) & (pos_row[other] < pos_col[k]) & ahead_lane
            rank_col = rank_col + jnp.sum(jnp.where(before, 1.0, 0.0), axis=1, keepdims=True)
            before = (o_col == e_row) & (pos_col[other] < pos_row[k]) & ahead_sub
            rank_row = rank_row + jnp.sum(jnp.where(before, 1.0, 0.0), axis=0, keepdims=True)
        rank_col = rank_col.astype(I32)
        rank_row = rank_row.astype(I32)
        kept = (lax.broadcasted_iota(I32, (seq, 1), 0) < length) & (rank_col < cap)
        scol_ref[0, :, k : k + 1] = jnp.where(kept, e_col * cap + rank_col, -1)
        kept = (lax.broadcasted_iota(I32, (1, seq), 1) < length) & (rank_row < cap)
        srow_ref[0, k : k + 1, :] = jnp.where(kept, e_row * cap + rank_row, -1)


def route_slots(lengths, routes, order, cap):
    micro, seq, _ = routes.shape
    row = jnp.swapaxes(routes, 1, 2)

    def spec(*dims):
        return pl.BlockSpec((1,) + dims, lambda m, *_: (m, 0, 0))

    return pl.pallas_call(
        functools.partial(route_kernel, cap=cap),
        out_shape=(
            jax.ShapeDtypeStruct((micro, TOPK, seq), I32),
            jax.ShapeDtypeStruct((micro, seq, TOPK), I32),
        ),
        grid_spec=pltpu.PrefetchScalarGridSpec(
            num_scalar_prefetch=1,
            grid=(micro,),
            in_specs=[
                spec(TOPK, seq),
                spec(seq, TOPK),
                spec(1, TOPK * seq),
                spec(TOPK * seq, 1),
            ],
            out_specs=(spec(TOPK, seq), spec(seq, TOPK)),
        ),
        compiler_params=params(),
        cost_estimate=cost(0, 1 << 20),
    )(lengths, row, routes, order[:, None, :], order[:, :, None])


def slot_onehot(srow, first, count):
    seq = srow.shape[1]
    slots = lax.broadcasted_iota(I32, (count, seq), 0) + first
    hit = slots == srow[0:1, :]
    for k in range(1, TOPK):
        hit = hit | (slots == srow[k : k + 1, :])
    return jnp.where(hit, 1.0, 0.0).astype(BF16)


def token_onehot(scol, which, count):
    seq = scol.shape[0]
    slots = lax.broadcasted_iota(I32, (seq, count), 1)
    hit = slots == scol[:, which[0] : which[0] + 1]
    for k in which[1:]:
        hit = hit | (slots == scol[:, k : k + 1])
    return jnp.where(hit, 1.0, 0.0).astype(BF16)


def spread_kernel(srow_ref, rows_ref, *out_refs, cap):
    seq = srow_ref.shape[2]
    rows = rows_ref[...].reshape(seq, rows_ref.shape[-1])
    for e, out in enumerate(out_refs):
        out[0] = dot(slot_onehot(srow_ref[0], e * cap, cap), rows).astype(BF16)


def spread_rows(srow, dealt, experts, cap):
    dp, micro, rows, width = dealt.shape
    seq = dp * rows
    return pl.pallas_call(
        functools.partial(spread_kernel, cap=cap),
        out_shape=tuple(
            jax.ShapeDtypeStruct((micro, cap, width), BF16) for _ in range(experts)
        ),
        grid=(micro,),
        in_specs=[
            pl.BlockSpec((1, TOPK, seq), lambda m: (m, 0, 0)),
            pl.BlockSpec((dp, 1, rows, width), lambda m: (0, m, 0, 0)),
        ],
        out_specs=tuple(
            pl.BlockSpec((1, cap, width), lambda m: (m, 0, 0)) for _ in range(experts)
        ),
        compiler_params=params(),
        cost_estimate=cost(4 * experts * cap * seq * width, 8 * micro * seq * width),
    )(srow, dealt)


def bias_kernel(line_ref, out_ref):
    seq = out_ref.shape[1]

    @pl.loop(0, out_ref.shape[0])
    def _(h):
        line = jnp.broadcast_to(line_ref[pl.ds(h, 1), :], (seq, 2 * seq))
        turned = pltpu.roll(line, seq + 1, 1, stride=1, stride_axis=0)
        out_ref[h] = turned[:, :seq].astype(BF16)


def bias_table(line):
    heads, wide = line.shape
    seq = wide // 2
    return pl.pallas_call(
        bias_kernel,
        out_shape=jax.ShapeDtypeStruct((heads, seq, seq), BF16),
        in_specs=[VM],
        out_specs=VM,
        compiler_params=params(),
        cost_estimate=cost(0, 4 * heads * seq * seq),
    )(line)


def norm_scale(v):
    return lax.rsqrt(jnp.mean(v * v, axis=-1, keepdims=True) + EPSILON)


def forward_kernel(
    len_ref, x_ref, w_ref, rows_ref, bias_ref, srow_ref, *refs, micro, experts, cap, carried
):
    refs = refs[carried:]
    qkv_ref, p_ref, o_ref, hres_ref, n2_ref, probs_ref = refs[:6]
    y_refs = refs[6:]
    length = len_ref[micro]
    seq, width = o_ref.shape[1], o_ref.shape[2]
    x = x_ref[...].reshape(seq, width).astype(F32)
    n1 = (x * norm_scale(x) * rows_ref[experts : experts + 1, :]).astype(BF16)
    for c in range(3):
        cols = slice(c * width, (c + 1) * width)
        qkv_ref[0, :, cols] = dot(n1, w_ref[:, cols]).astype(BF16)
    head = width // HEADS
    pair = 2 * head
    scale = 1.0 / math.sqrt(head)
    inside = lax.broadcasted_iota(I32, (seq, seq), 1) < length
    low = lax.broadcasted_iota(I32, (seq, pair), 1) < head

    @pl.loop(0, HEADS // 2)
    def _(hp):
        q2 = qkv_ref[0, :, pl.ds(pl.multiple_of(hp * pair, pair), pair)]
        k2 = qkv_ref[0, :, pl.ds(pl.multiple_of(width + hp * pair, pair), pair)]
        v2 = qkv_ref[0, :, pl.ds(pl.multiple_of(2 * width + hp * pair, pair), pair)]
        mixed = []
        for sub in range(2):
            mine = low if sub == 0 else jnp.logical_not(low)
            qm = jnp.where(mine, q2, jnp.zeros_like(q2))
            s = dot_nt(qm, k2) * scale + bias_ref[2 * hp + sub].astype(F32)
            s = jnp.where(inside, s, MASKED)
            e = jnp.exp(s - jnp.max(s, axis=-1, keepdims=True))
            p = (e * (1.0 / jnp.sum(e, axis=-1, keepdims=True))).astype(BF16)
            p_ref[0, 2 * hp + sub] = p
            mixed.append(dot(p, v2))
        o_ref[0, :, pl.ds(pl.multiple_of(hp * pair, pair), pair)] = jnp.where(
            low, mixed[0], mixed[1]
        ).astype(BF16)

    hres = x + dot(o_ref[0], w_ref[:, 3 * width : 4 * width])
    hres_ref[0] = hres
    n2 = (hres * norm_scale(hres) * rows_ref[experts + 1 : experts + 2, :]).astype(BF16)
    n2_ref[0] = n2
    logits = dot(n2, w_ref[:, 4 * width :])
    real = lax.broadcasted_iota(I32, logits.shape, 1) < experts
    logits = jnp.where(real, logits, -jnp.inf)
    e = jnp.exp(logits - jnp.max(logits, axis=-1, keepdims=True))
    probs_ref[0] = e * (1.0 / jnp.sum(e, axis=-1, keepdims=True))
    for r, y in enumerate(y_refs):
        y[...] = dot(slot_onehot(srow_ref[0], r * cap, cap), n2).astype(BF16)


def forward_step(micro, lengths, dealt, w, small_rows, bias, srow, experts, cap, carried):
    dp, micros, rows, width = dealt.shape
    seq = dp * rows
    lanes = w.shape[1] - 4 * width
    kept = [
        ((micros, seq, 3 * width), BF16),
        ((micros, HEADS, seq, seq), BF16),
        ((micros, seq, width), BF16),
        ((micros, seq, width), F32),
        ((micros, seq, width), BF16),
        ((micros, seq, lanes), F32),
    ]

    def at(shape):
        zeros = (0,) * (len(shape) - 1)
        return pl.BlockSpec((1,) + shape[1:], lambda i: (micro,) + zeros)

    def whole(shape):
        zeros = (0,) * len(shape)
        return pl.BlockSpec(shape, lambda i: zeros, pipeline_mode=pl.Buffered(1))

    out_shape = tuple(jax.ShapeDtypeStruct(s, d) for s, d in kept) + tuple(
        jax.ShapeDtypeStruct((cap, width), BF16) for _ in range(experts)
    )
    flops = 2 * seq * width * (4 * width + experts * cap) + 4 * HEADS * seq * seq * width // 4
    return pl.pallas_call(
        functools.partial(
            forward_kernel, micro=micro, experts=experts, cap=cap, carried=len(carried)
        ),
        out_shape=out_shape,
        grid=(1,),
        in_specs=[
            SM,
            pl.BlockSpec((dp, 1, rows, width), lambda i: (0, micro, 0, 0)),
            whole(w.shape),
            whole(small_rows.shape),
            whole(bias.shape),
            pl.BlockSpec((1, TOPK, seq), lambda i: (micro, 0, 0)),
        ]
        + [ANY] * len(carried),
        out_specs=tuple(at(s) for s, _ in kept)
        + tuple(pl.BlockSpec((cap, width), lambda i: (0, 0)) for _ in range(experts)),
        input_output_aliases={6 + n: n for n in range(len(carried))},
        compiler_params=params(),
        cost_estimate=cost(flops, 2 * w.size + 8 * seq * width),
    )(lengths, dealt, w, small_rows, bias, srow, *carried)


def gather_kernel(own_ref, wsm_ref, *refs, groups, micro, experts):
    y_in, g_in = refs[: groups * micro], refs[groups * micro : groups * (micro + 1)]
    y_ref, yt_ref, de_ref = refs[groups * (micro + 1) :]
    cap = y_in[0].shape[0]
    for n, yi in enumerate(y_in):
        y = yi[...]
        g = g_in[n // micro][n % micro]
        logits = dot(y, wsm_ref[...])
        lane = lax.broadcasted_iota(I32, logits.shape, 1)
        logits = jnp.where(lane < experts, logits, -jnp.inf)
        e = jnp.exp(logits - jnp.max(logits, axis=-1, keepdims=True))
        mine = jnp.sum(jnp.where(lane == own_ref[0], e, 0.0), axis=-1, keepdims=True)
        weight = mine * (1.0 / jnp.sum(e, axis=-1, keepdims=True))
        y_ref[n * cap : (n + 1) * cap, :] = y
        de_ref[n * cap : (n + 1) * cap, :] = (g.astype(F32) * weight).astype(BF16)
    yt_ref[...] = y_ref[...].T


def gather_expert(own, wsm, y_list, g_list, experts):
    groups, micro = len(g_list), g_list[0].shape[0]
    cap, width = y_list[0].shape
    total = groups * micro * cap
    return pl.pallas_call(
        functools.partial(gather_kernel, groups=groups, micro=micro, experts=experts),
        out_shape=(
            jax.ShapeDtypeStruct((total, width), BF16),
            jax.ShapeDtypeStruct((width, total), BF16),
            jax.ShapeDtypeStruct((total, width), BF16),
        ),
        in_specs=[SM, VM] + [VM] * (groups * (micro + 1)),
        out_specs=(VM, VM, VM),
        compiler_params=params(),
        cost_estimate=cost(2 * total * width * 128, 10 * total * width),
    )(own, wsm, *y_list, *g_list)


GELU_C = math.sqrt(2.0 / math.pi)


def inner_kernel(sel_ref, y_ref, yt_ref, de_ref, wg_ref, wu_ref, wo_ref, *refs, carried, parts):
    refs = refs[carried:]
    hid_ref, dg_ref, du_ref = refs[:3]
    out_refs = refs[3:-1]
    scr = refs[-1]
    y = y_ref[...]
    gate = dot(y, wg_ref[0])
    up = dot(y, wu_ref[0])
    dhid = dot_nt(de_ref[...], wo_ref[0])
    t = jnp.tanh(GELU_C * (gate + 0.044715 * (gate * gate * gate)))
    half = 0.5 * (1.0 + t)
    act = gate * half
    slope = half + 0.5 * gate * (1.0 - t * t) * (GELU_C * (1.0 + 3.0 * 0.044715 * (gate * gate)))
    hid_ref[...] = (act * up).astype(BF16)
    dg = (dhid * up * slope).astype(BF16)
    du = (dhid * act).astype(BF16)
    dg_ref[...] = dg
    du_ref[...] = du
    shards, rows = scr.shape[1], scr.shape[2]
    scr[0] = dot(yt_ref[...], dg).astype(BF16).reshape(shards, rows, dg.shape[1])
    scr[1] = dot(yt_ref[...], du).astype(BF16).reshape(shards, rows, dg.shape[1])
    for q, out in enumerate(out_refs):
        for z in range(shards // parts):
            src = z * parts + lax.bitwise_xor(sel_ref[0], q)
            for n in range(2):
                out[z, n] = scr[n, src]


def inner_step(sel, y, yt, de, w_in, w_out, first, count, block, shards, parts, carried):
    total, width = y.shape
    ff = w_out.shape[1]
    nf = ff // block
    rows = width // shards

    def whole(a):
        return pl.BlockSpec(a.shape, lambda f: (0, 0), pipeline_mode=pl.Buffered(1))

    big = [((total, ff), BF16)] * 3
    out_shape = tuple(jax.ShapeDtypeStruct(s, d) for s, d in big) + tuple(
        jax.ShapeDtypeStruct((shards // parts, 2, rows, count * block), BF16)
        for _ in range(parts)
    )
    return pl.pallas_call(
        functools.partial(inner_kernel, carried=len(carried), parts=parts),
        out_shape=out_shape,
        grid=(count,),
        in_specs=[
            SM,
            whole(y),
            whole(yt),
            whole(de),
            pl.BlockSpec((1, width, block), lambda f: (0, 0, first + f)),
            pl.BlockSpec((1, width, block), lambda f: (0, 0, nf + first + f)),
            pl.BlockSpec((1, block, width), lambda f: (0, first + f, 0)),
        ]
        + [ANY] * len(carried),
        out_specs=tuple(pl.BlockSpec((total, block), lambda f: (0, first + f)) for _ in big)
        + tuple(
            pl.BlockSpec((shards // parts, 2, rows, block), lambda f: (0, 0, 0, f))
            for _ in range(parts)
        ),
        scratch_shapes=[pltpu.VMEM((2, shards, rows, block), BF16)],
        input_output_aliases={7 + n: n for n in range(len(carried))},
        compiler_params=params(),
        cost_estimate=cost(
            2 * total * width * block * 5 * count, count * block * width * 6 + 6 * total * width
        ),
    )(sel, y, yt, de, w_in, w_in, w_out, *carried)


def outer_kernel(sel_ref, hid_ref, de_ref, *refs, parts):
    out_refs = refs[:-1]
    scr = refs[-1]
    f = pl.program_id(0)
    shards, rows = scr.shape[0], scr.shape[1]
    scr[...] = dot_tn(hid_ref[...], de_ref[...]).astype(BF16).reshape(scr.shape)
    del f
    for q, out in enumerate(out_refs):
        for z in range(shards // parts):
            out[z] = scr[z * parts + lax.bitwise_xor(sel_ref[0], q)]


def outer_step(sel, hid, de, col, ncols, shards, parts):
    total, ff = hid.shape
    width = de.shape[1]
    cols = width // ncols
    rows = ff // shards
    halves = 2
    per = shards // halves
    return pl.pallas_call(
        functools.partial(outer_kernel, parts=parts),
        out_shape=tuple(
            jax.ShapeDtypeStruct((shards // parts, rows, cols), BF16) for _ in range(parts)
        ),
        grid=(halves,),
        in_specs=[
            SM,
            pl.BlockSpec((total, ff // halves), lambda f: (0, f)),
            pl.BlockSpec((total, cols), lambda f: (0, col)),
        ],
        out_specs=tuple(
            pl.BlockSpec((per // parts, rows, cols), lambda f: (f, 0, 0)) for _ in range(parts)
        ),
        scratch_shapes=[pltpu.VMEM((per, rows, cols), BF16)],
        compiler_params=params(),
        cost_estimate=cost(2 * total * ff * cols, 2 * total * ff + ff * cols * 2),
    )(sel, hid, de)


def back_kernel(*refs, nmat, groups, transposed):
    a_refs = refs[:nmat]
    w_refs = refs[nmat : 2 * nmat]
    out_refs = refs[2 * nmat :]
    mul = dot_nt if transposed else dot
    acc = mul(a_refs[0][...], w_refs[0][0])
    for n in range(1, nmat):
        acc = acc + mul(a_refs[n][...], w_refs[n][0])
    acc = acc.astype(BF16)
    g = pl.program_id(0)
    for r, out in enumerate(out_refs):

        @pl.when(g == r)
        def _(out=out):
            out[...] = acc.reshape(out.shape)


def back_rows(mats, w, width, groups, micro, transposed):
    total, ff = mats[0].shape
    rows = total // groups
    n = len(mats)
    shape = (micro, rows // micro, width)
    if transposed:
        w_specs = [
            pl.BlockSpec(
                (1, width, ff), lambda g, i=i: (0, 0, i), pipeline_mode=pl.Buffered(1)
            )
            for i in range(n)
        ]
    else:
        w_specs = [
            pl.BlockSpec((1, ff, width), lambda g: (0, 0, 0), pipeline_mode=pl.Buffered(1))
        ]
    return pl.pallas_call(
        functools.partial(back_kernel, nmat=n, groups=groups, transposed=transposed),
        out_shape=tuple(jax.ShapeDtypeStruct(shape, BF16) for _ in range(groups)),
        grid=(groups,),
        in_specs=[pl.BlockSpec((rows, ff), lambda g: (g, 0)) for _ in mats] + w_specs,
        out_specs=tuple(pl.BlockSpec(shape, lambda g: (0, 0, 0)) for _ in range(groups)),
        compiler_params=params(),
        cost_estimate=cost(2 * total * ff * width * n, n * (2 * total * ff + 2 * ff * width)),
    )(*mats, *([w] * n))


def combine_kernel(len_ref, scol_ref, probs_ref, hres_ref, cot_ref, *refs, experts, cap):
    eo_refs = refs[:experts]
    out_ref, dl_ref, eo_scr = refs[experts:]
    m = pl.program_id(0)
    seq, width = hres_ref.shape[1], hres_ref.shape[2]
    for r, eo in enumerate(eo_refs):
        eo_scr[r * cap : (r + 1) * cap, :] = eo[0]
    scol = scol_ref[0]
    valid = lax.broadcasted_iota(I32, (seq, 1), 0) < len_ref[m]
    up = jnp.where(valid, cot_ref[...].reshape(seq, width).astype(F32), 0.0)
    probs = probs_ref[0]
    lane = lax.broadcasted_iota(I32, probs.shape, 1)
    total = hres_ref[0]
    dprobs = jnp.zeros_like(probs)
    own = len_ref[len_ref.shape[0] - 1]
    for k in range(TOPK):
        slot = scol[:, k : k + 1]
        picked = dot(token_onehot(scol, (k,), experts * cap), eo_scr[...])
        kept = slot >= 0
        rel = jnp.zeros_like(slot)
        for r in range(1, experts):
            rel = rel + jnp.where(slot >= r * cap, 1, 0)
        e = lax.bitwise_xor(rel, own)
        here = (lane == e) & kept
        w = jnp.sum(jnp.where(here, probs, 0.0), axis=-1, keepdims=True)
        total = total + w * picked
        dw = jnp.sum(up * picked, axis=-1, keepdims=True)
        dprobs = dprobs + jnp.where(here, dw, 0.0)
    dl_ref[0] = probs * (dprobs - jnp.sum(probs * dprobs, axis=-1, keepdims=True))
    out_ref[...] = jnp.where(valid, total, 0.0).astype(BF16).reshape(out_ref.shape)


def combine(lens_own, scol, probs, hres, cot, eo_list, experts, cap):
    dp, micro, rows, width = cot.shape
    seq = dp * rows
    lanes = probs.shape[-1]

    def spec(*dims):
        return pl.BlockSpec((1,) + dims, lambda m: (m, 0, 0))

    return pl.pallas_call(
        functools.partial(combine_kernel, experts=experts, cap=cap),
        out_shape=(
            jax.ShapeDtypeStruct((dp, micro, rows, width), BF16),
            jax.ShapeDtypeStruct((micro, seq, lanes), F32),
        ),
        grid=(micro,),
        in_specs=[
            SM,
            spec(seq, TOPK),
            spec(seq, lanes),
            spec(seq, width),
            pl.BlockSpec((dp, 1, rows, width), lambda m: (0, m, 0, 0)),
        ]
        + [spec(cap, width) for _ in range(experts)],
        out_specs=(
            pl.BlockSpec((dp, 1, rows, width), lambda m: (0, m, 0, 0)),
            spec(seq, lanes),
        ),
        scratch_shapes=[pltpu.VMEM((experts * cap, width), BF16)],
        compiler_params=params(),
        cost_estimate=cost(
            4 * micro * seq * experts * cap * width, 20 * micro * seq * width
        ),
    )(lens_own, scol, probs, hres, cot, *eo_list)


def split_dot_tn(a, b):
    high = a.astype(BF16)
    rest = (a - high.astype(F32)).astype(BF16)
    return dot_tn(high, b) + dot_tn(rest, b)


def backward_kernel(
    len_ref, sel_ref, x_ref, w_ref, rows_ref, once_ref, scol_ref, qkv_ref, p_ref, o_ref,
    hres_ref, n2_ref, cot_ref, dl_ref, *refs, experts, cap, micro, low_bits,
):
    dy_refs = refs[:experts]
    dx_ref = refs[experts]
    nouts = len(refs) - experts - 1 - 9
    out_refs = refs[experts + 1 : experts + 1 + nouts]
    dy_scr, n1_scr, dqkv_scr, o_scr, da_scr, do_scr, small_scr, diag_scr, grad_scr = refs[
        experts + 1 + nouts :
    ]
    m = pl.program_id(0)
    seq, width = hres_ref.shape[1], hres_ref.shape[2]
    head = width // HEADS
    pair = 2 * head
    scale = 1.0 / math.sqrt(head)

    @pl.when(m == 0)
    def _():
        small_scr[...] = jnp.zeros_like(small_scr)
        diag_scr[...] = jnp.zeros_like(diag_scr)

    for r, dy in enumerate(dy_refs):
        dy_scr[r * cap : (r + 1) * cap, :] = dy[0]
    dl = dl_ref[0]
    valid = lax.broadcasted_iota(I32, (seq, 1), 0) < len_ref[m]
    up = jnp.where(valid, cot_ref[...].reshape(seq, width).astype(F32), 0.0)
    dn2 = dot(token_onehot(scol_ref[0], tuple(range(TOPK)), experts * cap), dy_scr[...])
    for e in range(experts):
        dn2 = dn2 + dl[:, e : e + 1] * rows_ref[e : e + 1, :]
    hres = hres_ref[0]
    r2 = norm_scale(hres)
    small_scr[experts + 1 : experts + 2, :] += jnp.sum(dn2 * (hres * r2), axis=0, keepdims=True)
    a2 = dn2 * rows_ref[experts + 1 : experts + 2, :]
    dh = up + r2 * a2 - hres * (r2 * r2 * r2 * jnp.mean(a2 * hres, axis=-1, keepdims=True))
    da = dh.astype(BF16)
    da_scr[pl.ds(m * seq, seq), :] = da
    o_scr[pl.ds(m * seq, seq), :] = o_ref[0]
    small_scr[0:experts, :] += split_dot_tn(dl, n2_ref[0])[0:experts, :]
    do_scr[...] = dot_nt(da, w_ref[:, 3 * width : 4 * width]).astype(BF16)
    low = lax.broadcasted_iota(I32, (seq, pair), 1) < head
    place = pl.ds(pl.multiple_of(m * seq, seq), seq)

    @pl.loop(0, HEADS // 2)
    def _(hp):
        lo = pl.multiple_of(hp * pair, pair)
        q2 = qkv_ref[0, :, pl.ds(lo, pair)]
        k2 = qkv_ref[0, :, pl.ds(pl.multiple_of(width + lo, pair), pair)]
        v2 = qkv_ref[0, :, pl.ds(pl.multiple_of(2 * width + lo, pair), pair)]
        do2 = do_scr[:, pl.ds(lo, pair)]
        dq, dk, dv = [], [], []
        for sub in range(2):
            mine = low if sub == 0 else jnp.logical_not(low)
            dom = jnp.where(mine, do2, jnp.zeros_like(do2))
            p = p_ref[0, 2 * hp + sub]
            pf = p.astype(F32)
            dp = dot_nt(dom, v2)
            ds = pf * (dp - jnp.sum(pf * dp, axis=-1, keepdims=True))
            dsb = ds.astype(BF16)
            dq.append(dot(dsb, k2))
            dk.append(dot_tn(dsb, q2))
            dv.append(dot_tn(p, do2))
            fold = jnp.concatenate([jnp.zeros((seq, seq), F32), ds], axis=1)
            n = seq // 2
            while n >= 8:
                fold = fold[:n] + pltpu.roll(fold[n:], 2 * seq - n, 1)
                n //= 2
            diag_scr[2 * hp + sub] += fold
        dqkv_scr[place, pl.ds(lo, pair)] = (jnp.where(low, dq[0], dq[1]) * scale).astype(BF16)
        dqkv_scr[place, pl.ds(pl.multiple_of(width + lo, pair), pair)] = (
            jnp.where(low, dk[0], dk[1]) * scale
        ).astype(BF16)
        dqkv_scr[place, pl.ds(pl.multiple_of(2 * width + lo, pair), pair)] = jnp.where(
            low, dv[0], dv[1]
        ).astype(BF16)

    dn1 = dot_nt(dqkv_scr[place, :], w_ref[:, 0 : 3 * width])
    x = x_ref[...].reshape(seq, width).astype(F32)
    r1 = norm_scale(x)
    gain = rows_ref[experts : experts + 1, :]
    n1_scr[place, :] = (x * r1 * gain).astype(BF16)
    small_scr[experts : experts + 1, :] += jnp.sum(dn1 * (x * r1), axis=0, keepdims=True)
    a1 = dn1 * gain
    dx = dh + r1 * a1 - x * (r1 * r1 * r1 * jnp.mean(a1 * x, axis=-1, keepdims=True))
    dx_ref[...] = dx.astype(BF16).reshape(dx_ref.shape)

    @pl.when(m == micro - 1)
    def _():
        shards, rows = grad_scr.shape[0], grad_scr.shape[1]
        n1t = n1_scr[...].T
        step = width // 2
        for c in range(6):
            cols = slice(c * step, (c + 1) * step)
            grad_scr[:, :, cols] = (
                dot(n1t, dqkv_scr[:, cols]).astype(BF16).reshape(shards, rows, step)
            )
        ot = o_scr[...].T
        for c in range(2):
            cols = slice(c * step, (c + 1) * step)
            grad_scr[:, :, 3 * width + c * step : 3 * width + (c + 1) * step] = (
                dot(ot, da_scr[:, cols]).astype(BF16).reshape(shards, rows, step)
            )
        lines = diag_scr[:, 7, :]
        for s in range(7):
            lines = lines + pltpu.roll(diag_scr[:, s, :], 7 - s, 1)
        high = lines.astype(BF16)
        mid = (lines - high.astype(F32)).astype(BF16)
        rest = (lines - high.astype(F32) - mid.astype(F32)).astype(BF16)
        once = once_ref[...]
        buckets = dot_nt(once, high) + dot_nt(once, mid) + dot_nt(once, rest)
        lanes = w_ref.shape[1] - 4 * width
        per = NB * HEADS // shards
        sub = lax.broadcasted_iota(I32, (width, HEADS), 0)
        col = lax.broadcasted_iota(I32, (width, HEADS), 1)
        flat = div2(sub, rows) * per + mod2(sub, rows)
        row_bucket = lax.broadcasted_iota(I32, (width, NB), 1)
        flat_b = lax.broadcasted_iota(I32, (width, NB), 0)
        flat_b = div2(flat_b, rows) * per + mod2(flat_b, rows)
        pick = jnp.where(row_bucket == div2(flat_b, HEADS), 1.0, 0.0).astype(BF16)
        bh = buckets.astype(BF16)
        bm = (buckets - bh.astype(F32)).astype(BF16)
        spread = dot(pick, bh) + dot(pick, bm)
        mine = (col == mod2(flat, HEADS)) & (mod2(sub, rows) < per)
        bias_col = jnp.sum(jnp.where(mine, spread, 0.0), axis=1, keepdims=True)
        cols = small_scr[...].T
        lane = lax.broadcasted_iota(I32, (width, lanes), 1)
        tail = jnp.where(lane == experts + 2, bias_col, jnp.zeros((width, lanes), F32))
        tail = tail + jnp.concatenate(
            [cols, jnp.zeros((width, lanes - cols.shape[1]), F32)], axis=1
        )
        grad_scr[:, :, 4 * width :] = tail.astype(BF16).reshape(shards, rows, lanes)
        base = 0
        per_out = 1 << low_bits
        for out in out_refs:
            count = out.shape[0]
            high_n = out.shape[1]
            for low_pos in range(count):
                at = lax.bitwise_xor(sel_ref[0], base + low_pos)
                for z in range(high_n):
                    out[low_pos, z] = grad_scr[z * per_out + at]
            base += count


def backward(
    lens, sel, dealt, w, small_rows, once, scol, kept, cot, dl, dy_list, experts, cap, shards,
    low_bits, low_counts,
):
    qkv, p, o, hres, n2 = kept
    dp, micro, rows, width = dealt.shape
    seq = dp * rows
    lanes = dl.shape[-1]
    high_n = shards >> low_bits
    srows = width // shards
    cols = w.shape[1]

    def spec(*dims):
        zeros = (0,) * len(dims)
        return pl.BlockSpec((1,) + dims, lambda m: (m,) + zeros)

    def whole(shape):
        zeros = (0,) * len(shape)
        return pl.BlockSpec(shape, lambda m: zeros, pipeline_mode=pl.Buffered(1))

    dealt_spec = pl.BlockSpec((dp, 1, rows, width), lambda m: (0, m, 0, 0))
    outs = [(c, high_n, srows, cols) for c in low_counts]
    total = micro * seq
    flops = 2 * total * width * (8 * width + experts * cap) + 12 * HEADS * micro * seq * seq * 128
    return pl.pallas_call(
        functools.partial(
            backward_kernel, experts=experts, cap=cap, micro=micro, low_bits=low_bits
        ),
        out_shape=(jax.ShapeDtypeStruct(dealt.shape, BF16),)
        + tuple(jax.ShapeDtypeStruct(s, BF16) for s in outs),
        grid=(micro,),
        in_specs=[
            SM,
            SM,
            dealt_spec,
            whole(w.shape),
            whole(small_rows.shape),
            whole(once.shape),
            spec(seq, TOPK),
            spec(seq, 3 * width),
            spec(HEADS, seq, seq),
            spec(seq, width),
            spec(seq, width),
            spec(seq, width),
            dealt_spec,
            spec(seq, lanes),
        ]
        + [spec(cap, width) for _ in range(experts)],
        out_specs=(dealt_spec,)
        + tuple(pl.BlockSpec(s, lambda m: (0, 0, 0, 0), pipeline_mode=pl.Buffered(1)) for s in outs),
        scratch_shapes=[
            pltpu.VMEM((experts * cap, width), BF16),
            pltpu.VMEM((total, width), BF16),
            pltpu.VMEM((total, 3 * width), BF16),
            pltpu.VMEM((total, width), BF16),
            pltpu.VMEM((total, width), BF16),
            pltpu.VMEM((seq, width), BF16),
            pltpu.VMEM((-(-(experts + 2) // 8) * 8, width), F32),
            pltpu.VMEM((HEADS, 8, 2 * seq), F32),
            pltpu.VMEM((shards, srows, cols), BF16),
        ],
        compiler_params=params(),
        cost_estimate=cost(flops, 2 * w.size * 2 + 20 * total * width),
    )(lens, sel, dealt, w, small_rows, once, scol, qkv, p, o, hres, n2, cot, dl, *dy_list)


def exchange(arrays, fast):
    if fast:
        n = len(arrays)
        out = [arrays[0]]
        for r in range(1, n):
            out.append(lax.ppermute(arrays[r], "expert", [(i, i ^ r) for i in range(n)]))
        return out
    stacked = jnp.stack(arrays)
    moved = lax.all_to_all(stacked, "expert", split_axis=0, concat_axis=0, tiled=True)
    return [moved[r] for r in range(len(arrays))]


def shards(
    inputs,
    cotangent,
    seq_lengths,
    deal_perm,
    routes,
    route_order,
    qkv_weight,
    out_weight,
    attention_gain,
    expert_gain,
    router_weight,
    position_bias,
    expert_in,
    expert_out,
):
    dp_count = lax.axis_size("dp")
    ex_count = lax.axis_size("expert")
    dp_index = lax.axis_index("dp")
    ex_index = lax.axis_index("expert")
    fast = dp_count == 8 and ex_count == 4
    micro, rows, width = deal_perm.shape[0], inputs.shape[1], inputs.shape[2]
    seq = rows * dp_count
    experts = router_weight.shape[1]
    cap = (5 * seq + 2 * experts - 1) // (2 * experts)
    nshards = dp_count * ex_count
    srows = qkv_weight.shape[0]
    per = position_bias.shape[0]
    base = ex_index if fast else jnp.zeros_like(ex_index)

    chosen = jnp.arange(micro, dtype=I32)[:, None] * dp_count + deal_perm
    order = chosen.T.reshape(-1)

    def deal(a):
        picked = pick_blocks(order, a).reshape(dp_count, micro, rows, width)
        return lax.all_to_all(picked, "dp", split_axis=0, concat_axis=0, tiled=True)

    def home(a):
        moved = lax.all_to_all(a, "dp", split_axis=0, concat_axis=0, tiled=True)
        return place_blocks(order, moved.reshape(micro * dp_count, rows, width))

    lanes = 128
    packed = jnp.concatenate(
        [
            qkv_weight,
            out_weight,
            router_weight,
            attention_gain[:, None],
            expert_gain[:, None],
            jnp.pad(position_bias, (0, srows - per))[:, None],
            jnp.zeros((srows, lanes - experts - 3), BF16),
        ],
        axis=1,
    )
    dealt = deal(inputs)
    w = lax.all_gather(packed, ("dp", "expert"), axis=0, tiled=True)
    dealt_cot = deal(cotangent)

    own_perm = lax.dynamic_index_in_dim(deal_perm, dp_index, 1, keepdims=False)
    lengths = seq_lengths[jnp.arange(micro, dtype=I32) * dp_count + own_perm]
    srow, scol = route_slots(lengths, lax.bitwise_xor(routes, base), route_order, cap)
    g_list = exchange(list(spread_rows(srow, dealt_cot, experts, cap)), fast)

    wsm = w[:, 4 * width :]
    srows8 = -(-(experts + 2) // 8) * 8
    small_rows = wsm.T[:srows8].astype(F32)
    table = wsm[:, experts + 2].reshape(nshards, srows)[:, :per].reshape(NB, HEADS)
    onehot = bucket_of_offsets(seq, NB, MAXDIST)
    line = jnp.dot(table.T, jnp.asarray(onehot, BF16), preferred_element_type=F32)
    bias = bias_table(line)

    kept = ()
    y_by_micro = []
    for m in range(micro):
        res = forward_step(m, lengths, dealt, w, small_rows, bias, srow, experts, cap, kept)
        kept = res[:6]
        y_by_micro.append(exchange(list(res[6:]), fast))
    qkv, probs_att, o, hres, n2, probs = kept

    own = ex_index.reshape(1).astype(I32)
    y_list = [y_by_micro[m][r] for r in range(experts) for m in range(micro)]
    y, yt, de = gather_expert(own, wsm, y_list, g_list, experts)

    block = 256
    nf = expert_out.shape[1] // block
    chunks = (3, 3, 3, 2)
    zero = jnp.zeros((1,), I32)
    sel, parts = zero, 1
    carried = ()
    in_parts = []
    first = 0
    for count in chunks:
        res = inner_step(
            sel, y, yt, de, expert_in, expert_out, first, count, block, dp_count, parts, carried
        )
        carried = res[:3]
        in_parts.append(res[3:])
        first += count
    assert first == nf
    hid, dgate, dup = carried
    ncols = 2
    out_parts = [outer_step(sel, hid, de, c, ncols, dp_count, parts) for c in range(ncols)]
    eo_list = exchange(list(back_rows([hid], expert_out, width, experts, micro, False)), fast)
    dy_list = exchange(list(back_rows([dgate, dup], expert_in, width, experts, micro, True)), fast)

    def reduce_dp(pieces):
        return lax.psum_scatter(pieces[0], "dp", scatter_dimension=0, tiled=True)[0]

    in_sums = [reduce_dp(p).astype(F32) for p in in_parts]
    out_sums = [reduce_dp(p).astype(F32) for p in out_parts]
    grad_in = jnp.concatenate([s[n] for n in range(2) for s in in_sums], axis=1)[None]
    grad_out = jnp.concatenate(out_sums, axis=1)[None]

    lens_own = jnp.concatenate([lengths, base.reshape(1).astype(I32)])
    block_out, dl = combine(lens_own, scol, probs, hres, dealt_cot, eo_list, experts, cap)
    output = home(block_out)

    back_once = jnp.asarray(np.roll(onehot, 8, axis=1), BF16)
    res = backward(
        lengths, zero, dealt, w, small_rows, back_once, scol,
        (qkv, probs_att, o, hres, n2), dealt_cot, dl, dy_list, experts, cap, nshards,
        nshards.bit_length() - 1, (nshards,),
    )
    input_grad = home(res[0])
    grads = res[1].reshape(width, -1)
    own_grads = lax.psum_scatter(
        grads, ("dp", "expert"), scatter_dimension=0, tiled=True
    ).astype(F32)
    tail = own_grads[:, 4 * width :]
    return (
        output,
        input_grad,
        own_grads[:, : 3 * width],
        own_grads[:, 3 * width : 4 * width],
        tail[:, experts],
        tail[:, experts + 1],
        tail[:, :experts],
        tail[:per, experts + 2],
        grad_in,
        grad_out,
    )


def solution(mesh):
    in_specs = (
        P("expert", "dp", None),
        P("expert", "dp", None),
        P("expert"),
        P("expert", None),
        P(("dp", "expert"), None, None),
        P(("dp", "expert"), None),
        P(("dp", "expert"), None),
        P(("dp", "expert"), None),
        P(("dp", "expert")),
        P(("dp", "expert")),
        P(("dp", "expert"), None),
        P(("dp", "expert")),
        P("expert", None, None),
        P("expert", None, None),
    )
    out_specs = (
        P("expert", "dp", None),
        P("expert", "dp", None),
        P(("dp", "expert"), None),
        P(("dp", "expert"), None),
        P(("dp", "expert")),
        P(("dp", "expert")),
        P(("dp", "expert"), None),
        P(("dp", "expert")),
        P("expert", "dp", None),
        P("expert", "dp", None),
    )
    return jax.shard_map(shards, mesh=mesh, in_specs=in_specs, out_specs=out_specs, check_vma=False)
```

```python
import functools
import math

import jax
import jax.numpy as jnp
import numpy as np
from jax import lax
from jax.experimental import pallas as pl
from jax.experimental.pallas import tpu as pltpu
from jax.sharding import PartitionSpec as P


HEADS = 16
NB = 32
MAXDIST = 128
TOPK = 2
EPSILON = 1e-06
MASKED = -1000000000.0
VMEM_LIMIT = 60 * 1024 * 1024
UNROLL = 2
BF16 = jnp.bfloat16
F32 = jnp.float32
I32 = jnp.int32


def bucket_of_offsets(length, buckets, reach):
    offset = np.arange(2 * length) - (length - 1)
    half = buckets // 2
    exact = half // 2
    distance = np.abs(offset)
    spread = exact + (
        np.log(np.maximum(distance, 1) / exact) / np.log(reach / exact) * (half - exact)
    ).astype(np.int32)
    spread = np.minimum(spread, half - 1)
    table = (offset > 0).astype(np.int32) * half + np.where(distance < exact, distance, spread)
    onehot = (table[None, :] == np.arange(buckets)[:, None]).astype(np.float32)
    onehot[:, 2 * length - 1] = 0.0
    return onehot


def params(mib=None):
    limit = VMEM_LIMIT if mib is None else mib * 1024 * 1024
    return pltpu.CompilerParams(vmem_limit_bytes=limit)


def cost(flops, nbytes):
    return pl.CostEstimate(flops=int(flops), bytes_accessed=int(nbytes), transcendentals=0)


VM = pl.BlockSpec(memory_space=pltpu.VMEM)
SM = pl.BlockSpec(memory_space=pltpu.SMEM)
ANY = pl.BlockSpec(memory_space=pl.ANY)


def div2(v, n):
    return lax.shift_right_logical(v, jnp.full_like(v, n.bit_length() - 1))


def mod2(v, n):
    return lax.bitwise_and(v, jnp.full_like(v, n - 1))


def dot(a, b):
    return jnp.dot(a, b, preferred_element_type=F32)


def dot_nt(a, b):
    return lax.dot_general(a, b, (((1,), (1,)), ((), ())), preferred_element_type=F32)


def dot_tn(a, b):
    return lax.dot_general(a, b, (((0,), (0,)), ((), ())), preferred_element_type=F32)


def pick_kernel(own_ref, table_ref, src_ref, *refs):
    out_refs, sems = refs[:-1], refs[-1]
    count, micro = len(out_refs), out_refs[0].shape[0]
    copies = [
        pltpu.make_async_copy(
            src_ref.at[table_ref[m, lax.bitwise_xor(own_ref[0], q)]],
            out_refs[q].at[m],
            sems.at[q * micro + m],
        )
        for q in range(count)
        for m in range(micro)
    ]
    for c in copies:
        c.start()
    for c in copies:
        c.wait()


def pick_blocks(own, table, src):
    micro, count = table.shape
    return pl.pallas_call(
        pick_kernel,
        out_shape=tuple(
            jax.ShapeDtypeStruct((micro,) + src.shape[1:], src.dtype) for _ in range(count)
        ),
        in_specs=[SM, SM, ANY],
        out_specs=(VM,) * count,
        scratch_shapes=[pltpu.SemaphoreType.DMA((src.shape[0],))],
        compiler_params=params(),
        cost_estimate=cost(0, 4 * src.size),
    )(own, table, src)


def place_kernel(table_ref, src_ref, out_ref, sems):
    count, micro = src_ref.shape[:2]
    copies = [
        pltpu.make_async_copy(
            src_ref.at[a, m], out_ref.at[table_ref[m, a]], sems.at[a * micro + m]
        )
        for a in range(count)
        for m in range(micro)
    ]
    for c in copies:
        c.start()
    for c in copies:
        c.wait()


def place_blocks(table, src):
    count, micro, rows, width = src.shape
    total = micro * count
    return pl.pallas_call(
        place_kernel,
        out_shape=jax.ShapeDtypeStruct((total, rows, width), BF16),
        in_specs=[SM, VM],
        out_specs=ANY,
        scratch_shapes=[pltpu.SemaphoreType.DMA((total,))],
        compiler_params=params(),
        cost_estimate=cost(0, 4 * total * rows * width),
    )(table, src)


def gather_rows(own, parts, out_ref):
    for q, part in enumerate(parts):
        rows = part.shape[1]
        at = pl.multiple_of(lax.bitwise_xor(own, q) * rows, rows)
        out_ref[0, pl.ds(at, rows), :] = part[0]


def route_kernel(len_ref, er_ref, ec_ref, orow_ref, ocol_ref, srow_ref, scol_ref, *, cap):
    length = len_ref[pl.program_id(0)]
    seq = er_ref.shape[2]
    pairs = TOPK * seq
    order_row = orow_ref[0]
    order_col = ocol_ref[0]
    wide = (seq, pairs)
    tall = (pairs, seq)
    pos_col, pos_row = [], []
    for k in range(TOPK):
        pair = lax.broadcasted_iota(I32, wide, 0) * TOPK + k
        when = lax.broadcasted_iota(I32, wide, 1).astype(F32)
        pos_col.append(jnp.sum(jnp.where(order_row == pair, when, 0.0), axis=1, keepdims=True))
        pair = lax.broadcasted_iota(I32, tall, 1) * TOPK + k
        when = lax.broadcasted_iota(I32, tall, 0).astype(F32)
        pos_row.append(jnp.sum(jnp.where(order_col == pair, when, 0.0), axis=0, keepdims=True))
    square = (seq, seq)
    ahead_lane = lax.broadcasted_iota(I32, square, 1) < length
    ahead_sub = lax.broadcasted_iota(I32, square, 0) < length
    for k in range(TOPK):
        e_col = ec_ref[0, :, k : k + 1]
        e_row = er_ref[0, k : k + 1, :]
        rank_col = jnp.zeros((seq, 1), F32)
        rank_row = jnp.zeros((1, seq), F32)
        for other in range(TOPK):
            o_row = er_ref[0, other : other + 1, :]
            o_col = ec_ref[0, :, other : other + 1]
            before = (o_row == e_col) & (pos_row[other] < pos_col[k]) & ahead_lane
            rank_col = rank_col + jnp.sum(jnp.where(before, 1.0, 0.0), axis=1, keepdims=True)
            before = (o_col == e_row) & (pos_col[other] < pos_row[k]) & ahead_sub
            rank_row = rank_row + jnp.sum(jnp.where(before, 1.0, 0.0), axis=0, keepdims=True)
        rank_col = rank_col.astype(I32)
        rank_row = rank_row.astype(I32)
        kept = (lax.broadcasted_iota(I32, (seq, 1), 0) < length) & (rank_col < cap)
        scol_ref[0, :, k : k + 1] = jnp.where(kept, e_col * cap + rank_col, -1)
        kept = (lax.broadcasted_iota(I32, (1, seq), 1) < length) & (rank_row < cap)
        srow_ref[0, k : k + 1, :] = jnp.where(kept, e_row * cap + rank_row, -1)


def route_slots(lengths, routes, order, cap):
    micro, seq, _ = routes.shape
    row = jnp.swapaxes(routes, 1, 2)

    def spec(*dims):
        return pl.BlockSpec((1,) + dims, lambda m, *_: (m, 0, 0))

    return pl.pallas_call(
        functools.partial(route_kernel, cap=cap),
        out_shape=(
            jax.ShapeDtypeStruct((micro, TOPK, seq), I32),
            jax.ShapeDtypeStruct((micro, seq, TOPK), I32),
        ),
        grid_spec=pltpu.PrefetchScalarGridSpec(
            num_scalar_prefetch=1,
            grid=(micro,),
            in_specs=[
                spec(TOPK, seq),
                spec(seq, TOPK),
                spec(1, TOPK * seq),
                spec(TOPK * seq, 1),
            ],
            out_specs=(spec(TOPK, seq), spec(seq, TOPK)),
        ),
        compiler_params=params(),
        cost_estimate=cost(0, 1 << 20),
    )(lengths, row, routes, order[:, None, :], order[:, :, None])


def slot_onehot(srow, first, count):
    seq = srow.shape[1]
    slots = lax.broadcasted_iota(I32, (count, seq), 0) + first
    hit = slots == srow[0:1, :]
    for k in range(1, TOPK):
        hit = hit | (slots == srow[k : k + 1, :])
    return jnp.where(hit, 1.0, 0.0).astype(BF16)


def token_onehot(scol, which, count):
    seq = scol.shape[0]
    slots = lax.broadcasted_iota(I32, (seq, count), 1)
    hit = slots == scol[:, which[0] : which[0] + 1]
    for k in which[1:]:
        hit = hit | (slots == scol[:, k : k + 1])
    return jnp.where(hit, 1.0, 0.0).astype(BF16)


def spread_kernel(own_ref, srow_ref, *refs, cap, count):
    parts, rows_ref, out_refs = refs[:count], refs[count], refs[count + 1 :]
    gather_rows(own_ref[0], parts, rows_ref)
    rows = rows_ref[0]
    for e, out in enumerate(out_refs):
        out[0] = dot(slot_onehot(srow_ref[0], e * cap, cap), rows).astype(BF16)


def spread_rows(own, srow, parts, experts, cap):
    micro, rows, width = parts[0].shape
    seq = rows * len(parts)

    def spec(*dims):
        return pl.BlockSpec((1,) + dims, lambda m: (m, 0, 0))

    return pl.pallas_call(
        functools.partial(spread_kernel, cap=cap, count=len(parts)),
        out_shape=(jax.ShapeDtypeStruct((micro, seq, width), BF16),)
        + tuple(jax.ShapeDtypeStruct((micro, cap, width), BF16) for _ in range(experts)),
        grid=(micro,),
        in_specs=[SM, spec(TOPK, seq)] + [spec(rows, width) for _ in parts],
        out_specs=(spec(seq, width),) + tuple(spec(cap, width) for _ in range(experts)),
        compiler_params=params(),
        cost_estimate=cost(4 * experts * cap * seq * width, 8 * micro * seq * width),
    )(own, srow, *parts)


def flat_place(index, rows, per):
    return div2(index, rows) * per + mod2(index, rows)


def norm_scale(v):
    return lax.rsqrt(jnp.mean(v * v, axis=-1, keepdims=True) + EPSILON)


def prepare(sel_ref, onehot_ref, piece_refs, w_ref, rows_ref, bias_ref, sems, maps, offsets, srows, experts):
    copies = []
    for piece, places, offset in zip(piece_refs, maps, offsets):
        count = piece.shape[1]
        for place, differ in enumerate(places):
            row = lax.bitwise_xor(sel_ref[0], differ) * srows + offset
            copies.append(
                pltpu.make_async_copy(
                    piece.at[place],
                    w_ref.at[pl.ds(pl.multiple_of(row, count), count)],
                    sems.at[len(copies)],
                )
            )
    for c in copies:
        c.start()
    for c in copies:
        c.wait()
    width = w_ref.shape[0]
    small = w_ref[:, 4 * width :].astype(F32).T
    rows_ref[...] = small[: rows_ref.shape[0]]
    shards = width // srows
    per = NB * HEADS // shards
    head = lax.broadcasted_iota(I32, (HEADS, width), 0)
    index = lax.broadcasted_iota(I32, (HEADS, width), 1)
    here = (mod2(flat_place(index, srows, per), HEADS) == head) & (mod2(index, srows) < per)
    held = jnp.where(here, small[experts + 2 : experts + 3, :], 0.0).astype(BF16)
    index = lax.broadcasted_iota(I32, (width, NB), 0)
    pick = div2(flat_place(index, srows, per), HEADS) == lax.broadcasted_iota(I32, (width, NB), 1)
    table = dot(held, jnp.where(pick, 1.0, 0.0).astype(BF16)).astype(BF16)
    line = dot(table, onehot_ref[...])
    seq = bias_ref.shape[1]
    for h in range(HEADS):
        turned = pltpu.roll(
            jnp.broadcast_to(line[h : h + 1, :], (8, 2 * seq)), seq + 1, 1, stride=1, stride_axis=0
        )
        for g in range(0, seq, 16):
            block = [
                (pltpu.roll(turned, i, 1) if i else turned)[:, :seq] for i in (g, g + 8)
            ]
            bias_ref[h, g : g + 16, :] = jnp.concatenate(block, axis=0).astype(BF16)


def prepare_kernel(sel_ref, onehot_ref, *refs, count, **order):
    w_ref, rows_ref, bias_ref, sems = refs[count:]
    prepare(sel_ref, onehot_ref, refs[:count], w_ref, rows_ref, bias_ref, sems, **order)


def prepare_weights(sel, onehot, pieces, maps, offsets, srows, experts):
    cols = pieces[0].shape[2]
    shards = sum(len(p) * q.shape[1] for p, q in zip(maps, pieces))
    seq = onehot.shape[1] // 2
    small = -(-(experts + 2) // 8) * 8
    return pl.pallas_call(
        functools.partial(
            prepare_kernel, count=len(pieces), maps=maps, offsets=offsets, srows=srows,
            experts=experts,
        ),
        out_shape=(
            jax.ShapeDtypeStruct((shards, cols), BF16),
            jax.ShapeDtypeStruct((small, shards), F32),
            jax.ShapeDtypeStruct((HEADS, seq, seq), BF16),
        ),
        in_specs=[SM, VM] + [ANY] * len(pieces),
        out_specs=(VM, VM, VM),
        scratch_shapes=[pltpu.SemaphoreType.DMA((sum(len(p) for p in maps),))],
        compiler_params=params(),
        cost_estimate=cost(0, 4 * shards * cols),
    )(sel, onehot, *pieces)


def forward_kernel(
    len_ref, own_ref, srow_ref, w_ref, rows_ref, bias_ref, *refs, micro, experts, cap, count, carried
):
    parts = refs[:count]
    refs = refs[count + carried :]
    x_ref, qkv_ref, p_ref, o_ref, hres_ref, n2_ref, probs_ref = refs[:7]
    y_refs = refs[7:]
    length = len_ref[micro]
    seq, width = o_ref.shape[1], o_ref.shape[2]
    gather_rows(own_ref[0], parts, x_ref)
    x = x_ref[0].astype(F32)
    n1 = (x * norm_scale(x) * rows_ref[experts : experts + 1, :]).astype(BF16)
    for c in range(3):
        cols = slice(c * width, (c + 1) * width)
        qkv_ref[0, :, cols] = dot(n1, w_ref[:, cols]).astype(BF16)
    head = width // HEADS
    pair = 2 * head
    scale = 1.0 / math.sqrt(head)
    inside = lax.broadcasted_iota(I32, (seq, seq), 1) < length
    low = lax.broadcasted_iota(I32, (seq, pair), 1) < head

    @pl.loop(0, HEADS // 2, unroll=UNROLL)
    def _(hp):
        q2 = qkv_ref[0, :, pl.ds(pl.multiple_of(hp * pair, pair), pair)]
        k2 = qkv_ref[0, :, pl.ds(pl.multiple_of(width + hp * pair, pair), pair)]
        v2 = qkv_ref[0, :, pl.ds(pl.multiple_of(2 * width + hp * pair, pair), pair)]
        mixed = []
        for sub in range(2):
            mine = low if sub == 0 else jnp.logical_not(low)
            qm = jnp.where(mine, q2, jnp.zeros_like(q2))
            s = dot_nt(qm, k2) * scale + bias_ref[2 * hp + sub].astype(F32)
            s = jnp.where(inside, s, MASKED)
            e = jnp.exp(s - jnp.max(s, axis=-1, keepdims=True))
            p = (e * (1.0 / jnp.sum(e, axis=-1, keepdims=True))).astype(BF16)
            p_ref[0, 2 * hp + sub] = p
            mixed.append(dot(p, v2))
        o_ref[0, :, pl.ds(pl.multiple_of(hp * pair, pair), pair)] = jnp.where(
            low, mixed[0], mixed[1]
        ).astype(BF16)

    hres = x + dot(o_ref[0], w_ref[:, 3 * width : 4 * width])
    hres_ref[0] = hres
    n2 = (hres * norm_scale(hres) * rows_ref[experts + 1 : experts + 2, :]).astype(BF16)
    n2_ref[0] = n2
    logits = dot(n2, w_ref[:, 4 * width :])
    real = lax.broadcasted_iota(I32, logits.shape, 1) < experts
    logits = jnp.where(real, logits, -jnp.inf)
    e = jnp.exp(logits - jnp.max(logits, axis=-1, keepdims=True))
    probs_ref[0] = e * (1.0 / jnp.sum(e, axis=-1, keepdims=True))
    for r, y in enumerate(y_refs):
        y[...] = dot(slot_onehot(srow_ref[0], r * cap, cap), n2).astype(BF16)


def forward_step(micro, lengths, own, parts, srow, w, small_rows, bias, experts, cap, carried):
    micros, rows, width = parts[0].shape
    seq = rows * len(parts)
    lanes = w.shape[1] - 4 * width
    kept = [
        ((micros, seq, width), BF16),
        ((micros, seq, 3 * width), BF16),
        ((micros, HEADS, seq, seq), BF16),
        ((micros, seq, width), BF16),
        ((micros, seq, width), F32),
        ((micros, seq, width), BF16),
        ((micros, seq, lanes), F32),
    ]

    def at(shape):
        zeros = (0,) * (len(shape) - 1)
        return pl.BlockSpec((1,) + shape[1:], lambda i: (micro,) + zeros)

    def whole(shape):
        zeros = (0,) * len(shape)
        return pl.BlockSpec(shape, lambda i: zeros, pipeline_mode=pl.Buffered(1))

    flops = 2 * seq * width * (4 * width + experts * cap) + 4 * HEADS * seq * seq * width // 4
    return pl.pallas_call(
        functools.partial(
            forward_kernel, micro=micro, experts=experts, cap=cap, count=len(parts),
            carried=len(carried),
        ),
        out_shape=tuple(jax.ShapeDtypeStruct(s, d) for s, d in kept)
        + tuple(jax.ShapeDtypeStruct((cap, width), BF16) for _ in range(experts)),
        grid=(1,),
        in_specs=[
            SM,
            SM,
            pl.BlockSpec((1, TOPK, seq), lambda i: (micro, 0, 0)),
            whole(w.shape),
            whole(small_rows.shape),
            whole(bias.shape),
        ]
        + [at(part.shape) for part in parts]
        + [ANY] * len(carried),
        out_specs=tuple(at(s) for s, _ in kept)
        + tuple(pl.BlockSpec((cap, width), lambda i: (0, 0)) for _ in range(experts)),
        input_output_aliases={6 + len(parts) + n: n for n in range(len(carried))},
        compiler_params=params(),
        cost_estimate=cost(flops, 2 * w.size + 8 * seq * width),
    )(lengths, own, srow, w, small_rows, bias, *parts, *carried)


def gather_expert(own, wsm_ref, y_in, g_in, y_ref, yt_ref, de_ref, experts):
    micro = g_in[0].shape[0]
    cap = y_in[0].shape[0]
    for n, yi in enumerate(y_in):
        y = yi[...]
        g = g_in[n // micro][n % micro]
        logits = dot(y, wsm_ref[...])
        lane = lax.broadcasted_iota(I32, logits.shape, 1)
        logits = jnp.where(lane < experts, logits, -jnp.inf)
        e = jnp.exp(logits - jnp.max(logits, axis=-1, keepdims=True))
        mine = jnp.sum(jnp.where(lane == own, e, 0.0), axis=-1, keepdims=True)
        weight = mine * (1.0 / jnp.sum(e, axis=-1, keepdims=True))
        y_ref[n * cap : (n + 1) * cap, :] = y
        de_ref[n * cap : (n + 1) * cap, :] = (g.astype(F32) * weight).astype(BF16)
    yt_ref[...] = y_ref[...].T


GELU_C = math.sqrt(2.0 / math.pi)


def inner_kernel(sel_ref, wg_ref, wu_ref, wo_ref, *refs, carried, gathered, experts, maps):
    if gathered:
        wsm_ref, refs = refs[0], refs[1:]
        y_in, g_in = refs[: gathered[0]], refs[gathered[0] : sum(gathered)]
        y_ref, yt_ref, de_ref = refs[sum(gathered) : sum(gathered) + 3]
        refs = refs[sum(gathered) + 3 :]

        @pl.when(pl.program_id(0) == 0)
        def _():
            gather_expert(sel_ref[1], wsm_ref, y_in, g_in, y_ref, yt_ref, de_ref, experts)
    else:
        y_ref, yt_ref, de_ref = refs[:3]
        refs = refs[3 + carried :]
    hid_ref, dg_ref, du_ref = refs[:3]
    out_refs = refs[3:-1]
    scr = refs[-1]
    y = y_ref[...]
    gate = dot(y, wg_ref[0])
    up = dot(y, wu_ref[0])
    dhid = dot_nt(de_ref[...], wo_ref[0])
    t = jnp.tanh(GELU_C * (gate + 0.044715 * (gate * gate * gate)))
    half = 0.5 * (1.0 + t)
    act = gate * half
    slope = half + 0.5 * gate * (1.0 - t * t) * (GELU_C * (1.0 + 3.0 * 0.044715 * (gate * gate)))
    hid_ref[...] = (act * up).astype(BF16)
    dg = (dhid * up * slope).astype(BF16)
    du = (dhid * act).astype(BF16)
    dg_ref[...] = dg
    du_ref[...] = du
    shards, rows = scr.shape[1], scr.shape[2]
    scr[0] = dot(yt_ref[...], dg).astype(BF16).reshape(shards, rows, dg.shape[1])
    scr[1] = dot(yt_ref[...], du).astype(BF16).reshape(shards, rows, dg.shape[1])
    for out, places in zip(out_refs, maps):
        for place, differ in enumerate(places):
            src = lax.bitwise_xor(sel_ref[0], differ)
            for n in range(2):
                out[place, n] = scr[n, src]


def inner_step(sel, rows_in, w_in, w_out, first, count, block, shards, maps, carried, gather=None):
    ff, width = w_out.shape[1:]
    nf = ff // block
    rows = width // shards

    def whole(shape):
        zeros = (0,) * len(shape)
        return pl.BlockSpec(shape, lambda f: zeros, pipeline_mode=pl.Buffered(1))

    if gather is None:
        total = rows_in[0].shape[0]
        given, gathered, experts = list(rows_in) + list(carried), (), 0
        given_specs = [whole(a.shape) for a in rows_in] + [ANY] * len(carried)
        made = []
    else:
        wsm, y_list, g_list, experts = gather
        total = sum(y.shape[0] for y in y_list)
        given, gathered = [wsm, *y_list, *g_list], (len(y_list), len(g_list))
        given_specs = [whole(a.shape) for a in given]
        made = [(total, width), (width, total), (total, width)]
    big = [((total, ff), BF16)] * 3
    return pl.pallas_call(
        functools.partial(
            inner_kernel, carried=len(carried), gathered=gathered, experts=experts, maps=maps
        ),
        out_shape=tuple(jax.ShapeDtypeStruct(s, BF16) for s in made)
        + tuple(jax.ShapeDtypeStruct(s, d) for s, d in big)
        + tuple(
            jax.ShapeDtypeStruct((len(places), 2, rows, count * block), BF16) for places in maps
        ),
        grid=(count,),
        in_specs=[
            SM,
            pl.BlockSpec((1, width, block), lambda f: (0, 0, first + f)),
            pl.BlockSpec((1, width, block), lambda f: (0, 0, nf + first + f)),
            pl.BlockSpec((1, block, width), lambda f: (0, first + f, 0)),
        ]
        + given_specs,
        out_specs=tuple(whole(s) for s in made)
        + tuple(pl.BlockSpec((total, block), lambda f: (0, first + f)) for _ in big)
        + tuple(
            pl.BlockSpec((len(places), 2, rows, block), lambda f: (0, 0, 0, f)) for places in maps
        ),
        scratch_shapes=[pltpu.VMEM((2, shards, rows, block), BF16)],
        input_output_aliases={7 + n: n for n in range(len(carried))},
        compiler_params=params(),
        cost_estimate=cost(
            2 * total * width * block * 5 * count, count * block * width * 6 + 6 * total * width
        ),
    )(sel, w_in, w_in, w_out, *given)


def outer_kernel(sel_ref, hid_ref, de_ref, *refs, maps):
    out_refs = refs[:-1]
    scr = refs[-1]
    f = pl.program_id(0)
    per = scr.shape[0]
    scr[...] = dot_tn(hid_ref[...], de_ref[...]).astype(BF16).reshape(scr.shape)
    for half in range(2):

        @pl.when(f == half)
        def _(half=half):
            for out, places in zip(out_refs, maps):
                for place, differ in enumerate(places):
                    if differ // per == half:
                        src = lax.bitwise_and(
                            lax.bitwise_xor(sel_ref[0], differ), jnp.int32(per - 1)
                        )
                        out[place] = scr[src]


def outer_step(sel, hid, de, col, ncols, shards, maps):
    total, ff = hid.shape
    width = de.shape[1]
    cols = width // ncols
    rows = ff // shards
    per = shards // 2
    shift = per.bit_length() - 1
    return pl.pallas_call(
        functools.partial(outer_kernel, maps=maps),
        out_shape=tuple(jax.ShapeDtypeStruct((len(p), rows, cols), BF16) for p in maps),
        grid_spec=pltpu.PrefetchScalarGridSpec(
            num_scalar_prefetch=1,
            grid=(2,),
            in_specs=[
                pl.BlockSpec(
                    (total, ff // 2),
                    lambda f, s: (0, lax.bitwise_xor(f, lax.shift_right_logical(s[0], shift))),
                ),
                pl.BlockSpec((total, cols), lambda f, s: (0, col)),
            ],
            out_specs=tuple(
                pl.BlockSpec((len(p), rows, cols), lambda f, s: (0, 0, 0)) for p in maps
            ),
            scratch_shapes=[pltpu.VMEM((per, rows, cols), BF16)],
        ),
        compiler_params=params(),
        cost_estimate=cost(2 * total * ff * cols, 2 * total * ff + ff * cols * 2),
    )(sel, hid, de)


def back_kernel(*refs, nmat, transposed):
    a_refs = refs[:nmat]
    w_refs = refs[nmat : 2 * nmat]
    out_refs = refs[2 * nmat :]
    mul = dot_nt if transposed else dot
    acc = mul(a_refs[0][...], w_refs[0][0])
    for n in range(1, nmat):
        acc = acc + mul(a_refs[n][...], w_refs[n][0])
    acc = acc.astype(BF16)
    g = pl.program_id(0)
    for r, out in enumerate(out_refs):

        @pl.when(g == r)
        def _(out=out):
            out[...] = acc.reshape(out.shape)


def back_rows(mats, w, width, groups, micro, transposed):
    total, ff = mats[0].shape
    rows = total // groups
    n = len(mats)
    shape = (micro, rows // micro, width)
    if transposed:
        w_specs = [
            pl.BlockSpec(
                (1, width, ff), lambda g, i=i: (0, 0, i), pipeline_mode=pl.Buffered(1)
            )
            for i in range(n)
        ]
    else:
        w_specs = [
            pl.BlockSpec((1, ff, width), lambda g: (0, 0, 0), pipeline_mode=pl.Buffered(1))
        ]
    return pl.pallas_call(
        functools.partial(back_kernel, nmat=n, transposed=transposed),
        out_shape=tuple(jax.ShapeDtypeStruct(shape, BF16) for _ in range(groups)),
        grid=(groups,),
        in_specs=[pl.BlockSpec((rows, ff), lambda g: (g, 0)) for _ in mats] + w_specs,
        out_specs=tuple(pl.BlockSpec(shape, lambda g: (0, 0, 0)) for _ in range(groups)),
        compiler_params=params(),
        cost_estimate=cost(2 * total * ff * width * n, n * (2 * total * ff + 2 * ff * width)),
    )(*mats, *([w] * n))


def combine_kernel(len_ref, own_ref, scol_ref, probs_ref, hres_ref, cot_ref, *refs, experts, cap):
    eo_refs = refs[:experts]
    out_ref, dl_ref, eo_scr = refs[experts:]
    m = pl.program_id(0)
    seq = hres_ref.shape[1]
    for r, eo in enumerate(eo_refs):
        eo_scr[r * cap : (r + 1) * cap, :] = eo[0]
    scol = scol_ref[0]
    valid = lax.broadcasted_iota(I32, (seq, 1), 0) < len_ref[m]
    up = jnp.where(valid, cot_ref[0].astype(F32), 0.0)
    probs = probs_ref[0]
    lane = lax.broadcasted_iota(I32, probs.shape, 1)
    total = hres_ref[0]
    dprobs = jnp.zeros_like(probs)
    for k in range(TOPK):
        slot = scol[:, k : k + 1]
        picked = dot(token_onehot(scol, (k,), experts * cap), eo_scr[...])
        kept = slot >= 0
        rel = jnp.zeros_like(slot)
        for r in range(1, experts):
            rel = rel + jnp.where(slot >= r * cap, 1, 0)
        e = lax.bitwise_xor(rel, own_ref[1])
        here = (lane == e) & kept
        w = jnp.sum(jnp.where(here, probs, 0.0), axis=-1, keepdims=True)
        total = total + w * picked
        dw = jnp.sum(up * picked, axis=-1, keepdims=True)
        dprobs = dprobs + jnp.where(here, dw, 0.0)
    dl_ref[0] = probs * (dprobs - jnp.sum(probs * dprobs, axis=-1, keepdims=True))
    out_ref[...] = jnp.where(valid, total, 0.0).astype(BF16).reshape(out_ref.shape)


def combine(lens, own, scol, probs, hres, cot, eo_list, experts, cap, count):
    micro, seq, width = cot.shape
    lanes = probs.shape[-1]
    rows = seq // count

    def spec(*dims):
        return pl.BlockSpec((1,) + dims, lambda m: (m, 0, 0))

    return pl.pallas_call(
        functools.partial(combine_kernel, experts=experts, cap=cap),
        out_shape=(
            jax.ShapeDtypeStruct((count, micro, rows, width), BF16),
            jax.ShapeDtypeStruct((micro, seq, lanes), F32),
        ),
        grid=(micro,),
        in_specs=[
            SM,
            SM,
            spec(seq, TOPK),
            spec(seq, lanes),
            spec(seq, width),
            spec(seq, width),
        ]
        + [spec(cap, width) for _ in range(experts)],
        out_specs=(
            pl.BlockSpec((count, 1, rows, width), lambda m: (0, m, 0, 0)),
            spec(seq, lanes),
        ),
        scratch_shapes=[pltpu.VMEM((experts * cap, width), BF16)],
        compiler_params=params(),
        cost_estimate=cost(
            4 * micro * seq * experts * cap * width, 20 * micro * seq * width
        ),
    )(lens, own, scol, probs, hres, cot, *eo_list)


def split_dot_tn(a, b):
    high = a.astype(BF16)
    rest = (a - high.astype(F32)).astype(BF16)
    return dot_tn(high, b) + dot_tn(rest, b)


def backward_kernel(
    len_ref, w_ref, rows_ref, scol_ref, x_ref, qkv_ref, p_ref, hres_ref, n2_ref, cot_ref,
    dl_ref, *refs, experts, cap, micro, carried,
):
    dy_refs = refs[:experts]
    refs = refs[experts + carried :]
    dx_ref, n1_ref, dqkv_ref, da_ref, small_ref, diag_ref, dy_scr, do_scr = refs
    seq, width = hres_ref.shape[1], hres_ref.shape[2]
    head = width // HEADS
    pair = 2 * head
    scale = 1.0 / math.sqrt(head)
    small_ref[...] = jnp.zeros_like(small_ref)
    for r, dy in enumerate(dy_refs):
        dy_scr[r * cap : (r + 1) * cap, :] = dy[0]
    dl = dl_ref[0]
    valid = lax.broadcasted_iota(I32, (seq, 1), 0) < len_ref[micro]
    up = jnp.where(valid, cot_ref[0].astype(F32), 0.0)
    dn2 = dot(token_onehot(scol_ref[0], tuple(range(TOPK)), experts * cap), dy_scr[...])
    for e in range(experts):
        dn2 = dn2 + dl[:, e : e + 1] * rows_ref[e : e + 1, :]
    hres = hres_ref[0]
    r2 = norm_scale(hres)
    small_ref[experts + 1 : experts + 2, :] = jnp.sum(dn2 * (hres * r2), axis=0, keepdims=True)
    a2 = dn2 * rows_ref[experts + 1 : experts + 2, :]
    dh = up + r2 * a2 - hres * (r2 * r2 * r2 * jnp.mean(a2 * hres, axis=-1, keepdims=True))
    da = dh.astype(BF16)
    da_ref[...] = da
    small_ref[0:experts, :] = split_dot_tn(dl, n2_ref[0])[0:experts, :]
    do_scr[...] = dot_nt(da, w_ref[:, 3 * width : 4 * width]).astype(BF16)
    low = lax.broadcasted_iota(I32, (seq, pair), 1) < head

    @pl.loop(0, HEADS // 2, unroll=1)
    def _(hp):
        lo = pl.multiple_of(hp * pair, pair)
        q2 = qkv_ref[0, :, pl.ds(lo, pair)]
        k2 = qkv_ref[0, :, pl.ds(pl.multiple_of(width + lo, pair), pair)]
        v2 = qkv_ref[0, :, pl.ds(pl.multiple_of(2 * width + lo, pair), pair)]
        do2 = do_scr[:, pl.ds(lo, pair)]
        dq, dk, dv = [], [], []
        for sub in range(2):
            mine = low if sub == 0 else jnp.logical_not(low)
            dom = jnp.where(mine, do2, jnp.zeros_like(do2))
            p = p_ref[0, 2 * hp + sub]
            pf = p.astype(F32)
            dp = dot_nt(dom, v2)
            ds = pf * (dp - jnp.sum(pf * dp, axis=-1, keepdims=True))
            dsb = ds.astype(BF16)
            dq.append(dot(dsb, k2))
            dk.append(dot_tn(dsb, q2))
            dv.append(dot_tn(p, do2))
            fold = jnp.concatenate([jnp.zeros((seq, seq), F32), ds], axis=1)
            n = seq // 2
            while n >= 8:
                fold = fold[:n] + pltpu.roll(fold[n:], 2 * seq - n, 1)
                n //= 2
            diag_ref[2 * hp + sub] = fold
        dqkv_ref[:, pl.ds(lo, pair)] = (jnp.where(low, dq[0], dq[1]) * scale).astype(BF16)
        dqkv_ref[:, pl.ds(pl.multiple_of(width + lo, pair), pair)] = (
            jnp.where(low, dk[0], dk[1]) * scale
        ).astype(BF16)
        dqkv_ref[:, pl.ds(pl.multiple_of(2 * width + lo, pair), pair)] = jnp.where(
            low, dv[0], dv[1]
        ).astype(BF16)

    dn1 = dot_nt(dqkv_ref[...], w_ref[:, 0 : 3 * width])
    x = x_ref[0].astype(F32)
    r1 = norm_scale(x)
    gain = rows_ref[experts : experts + 1, :]
    n1_ref[...] = (x * r1 * gain).astype(BF16)
    small_ref[experts : experts + 1, :] = jnp.sum(dn1 * (x * r1), axis=0, keepdims=True)
    a1 = dn1 * gain
    dx = dh + r1 * a1 - x * (r1 * r1 * r1 * jnp.mean(a1 * x, axis=-1, keepdims=True))
    dx_ref[...] = dx.astype(BF16).reshape(dx_ref.shape)


def backward_step(
    m, lens, w, small_rows, scol, kept, cot, dl, dy_list, experts, cap, count, carried
):
    micro, seq, width = cot.shape
    rows = seq // count
    small = -(-(experts + 2) // 8) * 8

    def at(shape):
        zeros = (0,) * (len(shape) - 1)
        return pl.BlockSpec((1,) + shape[1:], lambda i: (m,) + zeros)

    def whole(shape):
        zeros = (0,) * len(shape)
        return pl.BlockSpec(shape, lambda i: zeros, pipeline_mode=pl.Buffered(1))

    outs = [
        ((seq, width), BF16),
        ((seq, 3 * width), BF16),
        ((seq, width), BF16),
        ((small, width), F32),
        ((HEADS, 8, 2 * seq), F32),
    ]
    flops = 2 * seq * width * (4 * width + experts * cap) + 12 * HEADS * seq * seq * 128
    return pl.pallas_call(
        functools.partial(
            backward_kernel, experts=experts, cap=cap, micro=m, carried=len(carried)
        ),
        out_shape=(jax.ShapeDtypeStruct((count, micro, rows, width), BF16),)
        + tuple(jax.ShapeDtypeStruct(s, d) for s, d in outs),
        grid=(1,),
        in_specs=[SM, whole(w.shape), whole(small_rows.shape), at(scol.shape)]
        + [at(a.shape) for a in kept]
        + [at(cot.shape), at(dl.shape)]
        + [at((micro, cap, width)) for _ in range(experts)]
        + [ANY] * len(carried),
        out_specs=(pl.BlockSpec((count, 1, rows, width), lambda i: (0, m, 0, 0)),)
        + tuple(pl.BlockSpec(s, lambda i, n=len(s): (0,) * n) for s, _ in outs),
        scratch_shapes=[
            pltpu.VMEM((experts * cap, width), BF16),
            pltpu.VMEM((seq, width), BF16),
        ],
        input_output_aliases={6 + len(kept) + experts + n: n for n in range(len(carried))},
        compiler_params=params(40),
        cost_estimate=cost(flops, 2 * w.size + 20 * seq * width),
    )(lens, w, small_rows, scol, *kept, cot, dl, *dy_list, *carried)


def put_shards(sel_ref, scr, out_refs, maps):
    for out, places in zip(out_refs, maps):
        for place, differ in enumerate(places):
            out[place] = scr[lax.bitwise_xor(sel_ref[0], differ)]


def weights_kernel(sel_ref, *refs, micro, first, step, maps):
    n1_refs, dqkv_refs = refs[:micro], refs[micro : 2 * micro]
    out_refs = refs[2 * micro : -3]
    n1_scr, d_scr, grad_scr = refs[-3:]
    shards, rows = grad_scr.shape[0], grad_scr.shape[1]
    seq = n1_refs[0].shape[0]
    for m in range(micro):
        n1_scr[m * seq : (m + 1) * seq, :] = n1_refs[m][...]
        d_scr[m * seq : (m + 1) * seq, :] = dqkv_refs[m][:, first : first + d_scr.shape[1]]
    n1t = n1_scr[...].T
    for c in range(d_scr.shape[1] // step):
        cols = slice(c * step, (c + 1) * step)
        grad_scr[:, :, cols] = dot(n1t, d_scr[:, cols]).astype(BF16).reshape(shards, rows, step)
    put_shards(sel_ref, grad_scr, out_refs, maps)


def weights_part(sel, n1_list, dqkv_list, first, cols, shards, maps):
    micro = len(n1_list)
    seq, width = n1_list[0].shape
    rows = width // shards
    total = micro * seq
    return pl.pallas_call(
        functools.partial(weights_kernel, micro=micro, first=first, step=width // 2, maps=maps),
        out_shape=tuple(jax.ShapeDtypeStruct((len(p), rows, cols), BF16) for p in maps),
        in_specs=[SM] + [VM] * (2 * micro),
        out_specs=tuple(VM for _ in maps),
        scratch_shapes=[
            pltpu.VMEM((total, width), BF16),
            pltpu.VMEM((total, cols), BF16),
            pltpu.VMEM((shards, rows, cols), BF16),
        ],
        compiler_params=params(28),
        cost_estimate=cost(2 * total * width * cols, 2 * total * (width + cols) + 2 * width * cols),
    )(sel, *n1_list, *dqkv_list)


def rest_kernel(sel_ref, once_ref, o_ref, *refs, micro, experts, step, maps):
    da_refs, small_refs, diag_refs = (refs[i * micro : (i + 1) * micro] for i in range(3))
    out_refs = refs[3 * micro : -2]
    da_scr, grad_scr = refs[-2:]
    shards, rows = grad_scr.shape[0], grad_scr.shape[1]
    seq, width = da_refs[0].shape
    for m in range(micro):
        da_scr[m * seq : (m + 1) * seq, :] = da_refs[m][...]
    ot = o_ref[...].reshape(micro * seq, width).T
    for c in range(width // step):
        cols = slice(c * step, (c + 1) * step)
        grad_scr[:, :, cols] = dot(ot, da_scr[:, cols]).astype(BF16).reshape(shards, rows, step)
    lines = jnp.zeros((HEADS, diag_refs[0].shape[2]), F32)
    small = jnp.zeros(small_refs[0].shape, F32)
    for m in range(micro):
        for s in range(8):
            line = diag_refs[m][:, s, :]
            lines = lines + (pltpu.roll(line, 7 - s, 1) if s < 7 else line)
        small = small + small_refs[m][...]
    high = lines.astype(BF16)
    mid = (lines - high.astype(F32)).astype(BF16)
    last = (lines - high.astype(F32) - mid.astype(F32)).astype(BF16)
    once = once_ref[...]
    buckets = dot_nt(once, high) + dot_nt(once, mid) + dot_nt(once, last)
    lanes = grad_scr.shape[2] - width
    per = NB * HEADS // shards
    sub = lax.broadcasted_iota(I32, (width, HEADS), 0)
    col = lax.broadcasted_iota(I32, (width, HEADS), 1)
    flat = flat_place(sub, rows, per)
    row_bucket = lax.broadcasted_iota(I32, (width, NB), 1)
    flat_b = flat_place(lax.broadcasted_iota(I32, (width, NB), 0), rows, per)
    pick = jnp.where(row_bucket == div2(flat_b, HEADS), 1.0, 0.0).astype(BF16)
    bh = buckets.astype(BF16)
    bm = (buckets - bh.astype(F32)).astype(BF16)
    spread = dot(pick, bh) + dot(pick, bm)
    mine = (col == mod2(flat, HEADS)) & (mod2(sub, rows) < per)
    bias_col = jnp.sum(jnp.where(mine, spread, 0.0), axis=1, keepdims=True)
    cols = small.T
    lane = lax.broadcasted_iota(I32, (width, lanes), 1)
    tail = jnp.where(lane == experts + 2, bias_col, jnp.zeros((width, lanes), F32))
    tail = tail + jnp.concatenate([cols, jnp.zeros((width, lanes - cols.shape[1]), F32)], axis=1)
    grad_scr[:, :, width:] = tail.astype(BF16).reshape(shards, rows, lanes)
    put_shards(sel_ref, grad_scr, out_refs, maps)


def rest_part(sel, once, o, da_list, small_list, diag_list, experts, lanes, shards, maps):
    micro = len(da_list)
    seq, width = da_list[0].shape
    rows = width // shards
    total = micro * seq
    cols = width + lanes
    return pl.pallas_call(
        functools.partial(
            rest_kernel, micro=micro, experts=experts, step=width // 2, maps=maps
        ),
        out_shape=tuple(jax.ShapeDtypeStruct((len(p), rows, cols), BF16) for p in maps),
        in_specs=[SM, VM, VM] + [VM] * (3 * micro),
        out_specs=tuple(VM for _ in maps),
        scratch_shapes=[
            pltpu.VMEM((total, width), BF16),
            pltpu.VMEM((shards, rows, cols), BF16),
        ],
        compiler_params=params(28),
        cost_estimate=cost(2 * total * width * width, 8 * total * width + 2 * width * cols),
    )(sel, once, o, *da_list, *small_list, *diag_list)


DP, EX = "dp", "expert"

CHUNKS = (3, 3, 3, 2)
DP_PLANS = ((1, 2, 4), (2, 1, 4), (1, 2, 4), (2, 1, 4), (1, 2, 4), (1, 2, 4))
ALL_PLANS = ((1, 2, 4, 8, 16), (1, 4, 2, 8, 16), (1, 8, 2, 4, 16))
GATHER_PLANS = ((16, 8, 4, 2, 1), (2, 16, 8, 4, 1))


def exchange(arrays, axis, fast):
    n = len(arrays)
    if fast:
        return [arrays[0]] + [
            lax.ppermute(arrays[r], axis, [(i, i ^ r) for i in range(n)]) for r in range(1, n)
        ]
    moved = lax.all_to_all(jnp.stack(arrays), axis, split_axis=0, concat_axis=0, tiled=True)
    return [moved[r] for r in range(n)]


def plus(*arrays):
    total = arrays[0].astype(F32)
    for a in arrays[1:]:
        total = total + a.astype(F32)
    return total


def differences(bits):
    places = (0,)
    for bit in reversed(bits):
        places = places + tuple(bit + p for p in places)
    return places


def maps_of(bits, count):
    if not bits:
        return (tuple(range(count)),)
    rest = differences(bits[1:])
    return rest, tuple(bits[0] + p for p in rest)


def reduce_halving(stay, give, moves):
    dims = (2,) * (len(moves) - 1)
    held = [stay.reshape(dims + stay.shape[1:])]
    send = give.reshape(dims + give.shape[1:])
    for n, move in enumerate(moves):
        if n:
            send = plus(*[h[1] for h in held]).astype(BF16)
            held = [h[0] for h in held]
        held.append(move(send))
    return plus(*held)


def shards(
    inputs,
    cotangent,
    seq_lengths,
    deal_perm,
    routes,
    route_order,
    qkv_weight,
    out_weight,
    attention_gain,
    expert_gain,
    router_weight,
    position_bias,
    expert_in,
    expert_out,
):
    dp_count, ex_count = lax.axis_size(DP), lax.axis_size(EX)
    dp_index, ex_index = lax.axis_index(DP), lax.axis_index(EX)
    fast = dp_count == 8 and ex_count == 4
    micro, rows, width = deal_perm.shape[0], inputs.shape[1], inputs.shape[2]
    seq = rows * dp_count
    experts = router_weight.shape[1]
    cap = (5 * seq + 2 * experts - 1) // (2 * experts)
    nshards = dp_count * ex_count
    srows = qkv_weight.shape[0]
    per = position_bias.shape[0]
    lanes = 128

    def flip(axis, size, bit):
        pairs = [(i, i ^ bit) for i in range(size)]
        return lambda a: lax.ppermute(a, axis, pairs)

    dp_moves = {bit: flip(DP, dp_count, bit) for bit in (1, 2, 4)}
    all_moves = {bit: flip(EX, ex_count, bit) for bit in (1, 2)}
    all_moves.update({bit * 4: move for bit, move in dp_moves.items()})

    def scalars(*values):
        return jnp.stack([v.astype(I32) if fast else jnp.zeros((), I32) for v in values])

    own = scalars(dp_index, ex_index)
    own_all = scalars(dp_index * ex_count + ex_index)
    own_dp = jnp.stack([own[0], ex_index.astype(I32)])
    table = jnp.arange(micro, dtype=I32)[:, None] * dp_count + deal_perm

    def deal(a):
        parts = pick_blocks(own, table, a)
        return exchange(list(parts), DP, fast)

    def home(part):
        moved = lax.all_to_all(part, DP, split_axis=0, concat_axis=0, tiled=True)
        return place_blocks(table, moved)

    packed = jnp.concatenate(
        [
            qkv_weight,
            out_weight,
            router_weight,
            attention_gain[:, None],
            expert_gain[:, None],
            jnp.pad(position_bias, (0, srows - per))[:, None],
            jnp.zeros((srows, lanes - experts - 3), BF16),
        ],
        axis=1,
    )
    if fast:
        half = srows // len(GATHER_PLANS)
        pieces, maps, offsets = [], [], []
        for n, bits in enumerate(GATHER_PLANS):
            held = packed[None, n * half : (n + 1) * half]
            places = (0,)
            for bit in bits[:-1]:
                held = jnp.concatenate([held, all_moves[bit](held)], axis=0)
                places = places + tuple(bit + p for p in places)
            other = all_moves[bits[-1]](held)
            pieces += [held, other]
            maps += [places, tuple(bits[-1] + p for p in places)]
            offsets += [n * half] * 2
    else:
        pieces = [lax.all_gather(packed, (DP, EX), axis=0, tiled=True)[None]]
        maps, offsets = [(0,)], [0]
    cot_parts = deal(cotangent)
    x_parts = deal(inputs)

    own_perm = lax.dynamic_index_in_dim(deal_perm, dp_index, 1, keepdims=False)
    lengths = seq_lengths[jnp.arange(micro, dtype=I32) * dp_count + own_perm]
    srow, scol = route_slots(lengths, lax.bitwise_xor(routes, own[1]), route_order, cap)
    cot, *g_list = spread_rows(own, srow, cot_parts, experts, cap)
    g_list = exchange(g_list, EX, fast)

    onehot = bucket_of_offsets(seq, NB, MAXDIST)
    w, small_rows, bias = prepare_weights(
        own_all, jnp.asarray(onehot, BF16), pieces, tuple(maps), tuple(offsets), srows, experts
    )
    kept = ()
    y_by_micro = []
    for m in range(micro):
        res = forward_step(m, lengths, own, x_parts, srow, w, small_rows, bias, experts, cap, kept)
        kept = res[:7]
        y_by_micro.append(exchange(list(res[7:]), EX, fast))
    x, qkv, probs_att, o, hres, n2, probs = kept

    y_list = [y_by_micro[m][r] for r in range(experts) for m in range(micro)]
    block = 256
    chunks = CHUNKS
    ncols = 2
    plans = DP_PLANS if fast else ((),) * len(DP_PLANS)

    def reduce_dp(pieces, number):
        if not fast:
            return lax.psum_scatter(pieces[0], DP, scatter_dimension=0, tiled=True)[0].astype(F32)
        moves = [dp_moves[bit] for bit in plans[number]]
        return reduce_halving(pieces[0], pieces[1], moves)

    rows_in = carried = ()
    gather = (w[:, 4 * width :], y_list, g_list, experts)
    in_sums = []
    first = 0
    for n, count in enumerate(chunks):
        res = inner_step(
            own_dp, rows_in, expert_in, expert_out, first, count, block, dp_count,
            maps_of(plans[n], dp_count), carried, gather,
        )
        if n == 0:
            rows_in, res, gather = res[:3], res[3:], None
        carried = res[:3]
        in_sums.append(reduce_dp(res[3:], n))
        first += count
    de = rows_in[2]
    hid, dgate, dup = carried
    eo_list = list(back_rows([hid], expert_out, width, experts, micro, False))
    eo_list = exchange(eo_list, EX, fast)
    dy_list = list(back_rows([dgate, dup], expert_in, width, experts, micro, True))
    dy_list = exchange(dy_list, EX, fast)
    out_sums = []
    for c in range(ncols):
        n = len(chunks) + c
        res = outer_step(own_dp, hid, de, c, ncols, dp_count, maps_of(plans[n], dp_count))
        out_sums.append(reduce_dp(res, n))
    block_out, dl = combine(lengths, own, scol, probs, hres, cot, eo_list, experts, cap, dp_count)
    output = home(block_out)

    dx = ()
    per_micro = []
    for m in range(micro):
        res = backward_step(
            m, lengths, w, small_rows, scol, (x, qkv, probs_att, hres, n2), cot, dl,
            dy_list, experts, cap, dp_count, dx,
        )
        dx = res[:1]
        per_micro.append(res[1:])
    n1_list, dqkv_list, da_list, small_list, diag_list = (list(v) for v in zip(*per_micro))
    dx = dx[0]

    def reduce_all(pieces, bits):
        if not fast:
            flat = pieces[0].reshape(width, -1)
            return lax.psum_scatter(flat, (DP, EX), scatter_dimension=0, tiled=True).astype(F32)
        return reduce_halving(pieces[0], pieces[1], [all_moves[bit] for bit in bits])

    grads = []
    cols_a = 3 * width // 2
    back_once = jnp.asarray(np.roll(onehot, 8, axis=1), BF16)
    for n, bits in enumerate(ALL_PLANS):
        places = maps_of(bits if fast else (), nshards)
        if n == 0:
            part = weights_part(own_all, n1_list, dqkv_list, 0, cols_a, nshards, places)
        elif n == 1:
            part = weights_part(
                own_all, n1_list, dqkv_list, cols_a, 3 * width - cols_a, nshards, places
            )
        else:
            part = rest_part(
                own_all, back_once, o, da_list, small_list, diag_list, experts, lanes, nshards,
                places,
            )
        grads.append(reduce_all(part, bits))
    if fast:
        in_sums[0], dx = lax.optimization_barrier((in_sums[0], dx))
    input_grad = home(dx)
    grad_in = jnp.concatenate([s[n] for n in range(2) for s in in_sums], axis=1)[None]
    grad_out = jnp.concatenate(out_sums, axis=1)[None]
    tail = grads[2][:, width:]
    return (
        output,
        input_grad,
        jnp.concatenate(grads[:2], axis=1),
        grads[2][:, :width],
        tail[:, experts],
        tail[:, experts + 1],
        tail[:, :experts],
        tail[:per, experts + 2],
        grad_in,
        grad_out,
    )


def solution(mesh):
    stored, both = P(EX, DP, None), (DP, EX)
    in_specs = (
        stored,
        stored,
        P(EX),
        P(EX, None),
        P(both, None, None),
        P(both, None),
        P(both, None),
        P(both, None),
        P(both),
        P(both),
        P(both, None),
        P(both),
        P(EX, None, None),
        P(EX, None, None),
    )
    out_specs = (
        stored,
        stored,
        P(both, None),
        P(both, None),
        P(both),
        P(both),
        P(both, None),
        P(both),
        stored,
        stored,
    )

    return jax.shard_map(shards, mesh=mesh, in_specs=in_specs, out_specs=out_specs, check_vma=False)
```
